32 devices in a mesh: ctx: 8 (over z, x), wsh: 4 (over y, core).
Axes of the slice: x: 2, y: 2, z: 4, core: 2. Of those that a mesh axis runs over, the one named last changes fastest.
Arguments:
- layer_input: bfloat16 [4, 2048, 1536], P('wsh', 'ctx'), may hold values from -6 to 6
- attention_gain: bfloat16 [1536], P('wsh'), may hold values from 0.099609375 to 1.8984375
- query_weight: bfloat16 [1536, 1536], P('wsh'), may hold values from -0.15625 to 0.15625
- key_matrix: bfloat16 [1536, 512], P('wsh'), may hold values from -0.15625 to 0.15625
- value_matrix: bfloat16 [1536, 512], P('wsh'), may hold values from -0.15625 to 0.15625
- output_weight: bfloat16 [1536, 1536], P('wsh'), may hold values from -1.25 to 1.25
- expert_gain: bfloat16 [1536], P('wsh'), may hold values from 0.099609375 to 1.8984375
- router_weight: bfloat16 [1536, 16], P('wsh'), may hold values from -0.078125 to 0.078125
- expert_inner: bfloat16 [16, 1536, 1024], P('ctx', 'wsh'), may hold values from -0.15625 to 0.15625
- expert_outer: bfloat16 [16, 512, 1536], P('ctx', 'wsh'), may hold values from -0.75 to 0.75
- document_lengths: int32 [4, 4], P('wsh'), may hold values from 1 to 1024, 1792 in all within a row
- token_places: int32 [4, 2048], P('wsh'), may hold values from 0 to 2047, each once within a row
- expert_routes: int32 [4, 2048, 8], P('wsh', 'ctx'), may hold values from 0 to 15, all different within a row; in each aligned block of 256 rows (0 to 255, 256 to 511, ..., all dimensions but the last counted through in order) at most 192 rows name the same one
- cotangent: bfloat16 [4, 2048, 1536], P('wsh', 'ctx'), may hold values from -6 to 6
Outputs:
- layer_output: bfloat16 [4, 2048, 1536], P('wsh', 'ctx')
- input_gradient: float32 [4, 2048, 1536], P('wsh', 'ctx')
- attention_gain_gradient: float32 [1536], P('wsh')
- query_weight_gradient: float32 [1536, 1536], P('wsh')
- key_weight_gradient: float32 [1536, 512], P('wsh')
- value_weight_gradient: float32 [1536, 512], P('wsh')
- output_weight_gradient: float32 [1536, 1536], P('wsh')
- expert_gain_gradient: float32 [1536], P('wsh')
- router_weight_gradient: float32 [1536, 16], P('wsh')
- expert_inner_gradient: float32 [16, 1536, 1024], P('ctx', 'wsh')
- expert_outer_gradient: float32 [16, 512, 1536], P('ctx', 'wsh')
The draws below stay inside these ranges and needn't reach their ends.
Inputs may be any that keep to these rules, and one draw needn't show every extreme that they name: `document_lengths`: each row holds the lengths of the 4 documents of one group in order; they sum to 1792, the longest is exactly 1024, and places from that sum on are pads. `token_places`: each row is a permutation of the places of one group. `expert_routes`: each token names 8 different experts. Among the 256 tokens of one device (aligned blocks of rows) no expert is named more than 192 times, a bound that some block reaches.
All inputs are finite; a program needn't handle non-finite values.
Results may differ from the reference program's by a relative error of at most 0.025.
Values may be sent and summed in bfloat16 or wider, within the bound.
A program may use at most 192 MiB of HBM per device.

```python
import math
import jax
import jax.numpy as jnp
import numpy as np
from jax import lax

MODEL_SIZE = 1536
QUERY_HEADS = 24
KEY_HEADS = 8
HEAD_SIZE = 64
EXPERT_H = 512
TOPK = 8
SEQS = 4
TOK_DEV = 256
EXPERTS = 16
GROUP_TOK = 2048
PAD_TOK = 256
MAX_LEN = 1024
CAP = 192
N_WSH = 4


def levels(key, extent, split, least, top_value):
    def one(position, blocks):
        draws = jax.random.uniform(jax.random.fold_in(jax.random.fold_in(key, 6), position), (blocks,), jnp.float32, least / len(split), top_value / len(split))
        return jnp.repeat(jnp.exp(draws), extent[position] // blocks).reshape((-1,) + (1,) * (len(extent) - position - 1))

    factor_of = one(*split[0])
    for cut in split[1:]:
        factor_of = factor_of * one(*cut)
    return factor_of


def profile(count, total, reach, skew):
    weights = [(1 << 20) // math.isqrt(standing ** skew) + 1 for standing in range(2, count + 1)]
    surplus, holding = total - reach - (count - 1), [1] * (count - 1)
    while surplus > 0:
        movable = [i for i in range(count - 1) if holding[i] < reach]
        mass, budget = sum([weights[i] for i in movable]), surplus
        for i in movable:
            addition = min(reach - holding[i], max(1, budget * weights[i] // mass), surplus)
            holding[i] = holding[i] + addition
            surplus = surplus - addition
    return np.array([reach] + holding)


def uneven(rng, number_of, total, most, skew):
    if number_of == 2:
        one = jax.random.randint(rng, (), max(1, total - most), min(most, total - 1) + 1)
        return jnp.stack([one, total - one])
    sizes = jnp.asarray(profile(number_of, total, most, skew), jnp.int32)
    pairs = (number_of - 1) // 2
    source_of, sink = sizes[1:1 + 2 * pairs:2], sizes[2:2 + 2 * pairs:2]
    slack = jnp.minimum(source_of - 1, most - sink)
    shifted = jax.random.randint(jax.random.fold_in(rng, 1), (pairs,), 0, 1 << 20) % (slack + 1)
    sizes = sizes.at[1:1 + 2 * pairs:2].set(source_of - shifted).at[2:2 + 2 * pairs:2].set(sink + shifted)
    return sizes[jax.random.permutation(jax.random.fold_in(rng, 2), number_of)]


def shared_out(own_key, own, number, rows, number_of, top, most, skew):
    sequence = jax.random.permutation(own_key, number_of)
    packed, common = shares(number_of, rows * top, most, skew, True), shares(number_of, rows * top, most, skew, False)
    places = jnp.arange(number_of)

    def named(sizes, rotation):
        used = int((sizes > 0).sum())
        fixed = max(1, used // 4)
        passed = fixed + (places - fixed + rotation * (used - fixed)) % max(1, number_of - fixed)
        return jnp.zeros((number_of,), jnp.int32).at[sequence[jnp.where(places < fixed, places, passed)]].set(jnp.asarray(sizes, jnp.int32))

    sizes = jnp.where(number % 4 == 0, named(packed, number // 4), named(common, number - number // 4 - 1))
    mixed = jax.random.permutation(jax.random.fold_in(own, 3), number_of)
    source_of, receiver = mixed[0:number_of // 2 * 2:2], mixed[1:number_of // 2 * 2:2]
    room = jnp.minimum(sizes[source_of] - 1, most - sizes[receiver]) // 2
    room = jnp.where((source_of == sequence[0]) | (receiver == sequence[0]) | (sizes[receiver] == 0), 0, jnp.maximum(room, 0))
    passed = jax.random.randint(jax.random.fold_in(own, 4), (number_of // 2,), 0, 1 << 20) % (room + 1)
    sizes = sizes.at[source_of].add(-passed).at[receiver].add(passed)
    labels = jnp.searchsorted(jnp.cumsum(sizes), jnp.arange(rows * top), side="right").astype(jnp.int32)
    table = labels.reshape(top, rows).T
    table = table[jax.random.permutation(jax.random.fold_in(own, 1), rows)]
    rotation = jax.random.randint(jax.random.fold_in(own, 2), (rows, 1), 0, top)
    return jnp.take_along_axis(table, (jnp.arange(top)[None, :] + rotation) % top, axis=1)


def shares(number_of, total, bound, skew, full):
    portions = [(1 << 20) // math.isqrt(rank ** skew) + 1 for rank in range(1, number_of + 1)]
    largest = bound if full else min(bound, max(-(-total // number_of), total * portions[0] // sum(portions)))
    least = 1 if total - largest >= number_of - 1 else 0
    given, rest = [largest] + [least] * (number_of - 1), total - largest - least * (number_of - 1)
    while rest > 0:
        candidates = [i for i in range(1, number_of) if given[i] < largest] or [i for i in range(1, number_of) if given[i] < bound]
        pool, remaining = sum([portions[i] for i in candidates]), rest
        for i in candidates:
            addition = min(bound - given[i], max(1, remaining * portions[i] // pool), rest)
            given[i] = given[i] + addition
            rest = rest - addition
    return np.array(given)


def bell_draw(stream_key, shape, width, reach, cuts=(), kind=jnp.bfloat16):
    values = width * jax.random.normal(stream_key, shape, jnp.float32)
    if cuts:
        values = values * levels(stream_key, shape, cuts, -0.22, 0.18)
    return jnp.clip(values, -reach, reach).astype(kind)


def setup_inputs(seed: int = 0) -> dict:
    seeds = jax.random.split(jax.random.key(seed), 15)
    layer_input = bell_draw(seeds[0], (N_WSH, GROUP_TOK, MODEL_SIZE), 1.0, 6.0, ((0, 4), (1, 8)))
    attention_gain = jnp.clip(1.0 + 0.18 * jax.random.normal(seeds[1], (MODEL_SIZE,), jnp.float32), 0.099609375, 1.8984375).astype(jnp.bfloat16)
    query_weight = bell_draw(seeds[2], (MODEL_SIZE, QUERY_HEADS * HEAD_SIZE), MODEL_SIZE ** -0.5, 0.15625, ((0, 4),))
    key_matrix = bell_draw(seeds[3], (MODEL_SIZE, KEY_HEADS * HEAD_SIZE), MODEL_SIZE ** -0.5, 0.15625, ((0, 4),))
    value_matrix = bell_draw(seeds[4], (MODEL_SIZE, KEY_HEADS * HEAD_SIZE), MODEL_SIZE ** -0.5, 0.15625, ((0, 4),))
    output_weight = bell_draw(seeds[5], (QUERY_HEADS * HEAD_SIZE, MODEL_SIZE), (QUERY_HEADS * HEAD_SIZE // 64) ** -0.5, 1.25, ((0, 4),))
    expert_gain = jnp.clip(1.0 + 0.18 * jax.random.normal(seeds[6], (MODEL_SIZE,), jnp.float32), 0.099609375, 1.8984375).astype(jnp.bfloat16)
    router_weight = bell_draw(seeds[7], (MODEL_SIZE, EXPERTS), (4 * MODEL_SIZE) ** -0.5, 0.078125, ((0, 4),))
    expert_inner = bell_draw(seeds[8], (EXPERTS, MODEL_SIZE, 2 * EXPERT_H), MODEL_SIZE ** -0.5, 0.15625, ((0, 8), (1, 4)))
    expert_outer = bell_draw(seeds[9], (EXPERTS, EXPERT_H, MODEL_SIZE), (EXPERT_H // 8) ** -0.5, 0.75, ((0, 8), (1, 4)))
    document_lengths = jax.vmap(lambda own: uneven(own, SEQS, GROUP_TOK - PAD_TOK, MAX_LEN, 2))(jax.random.split(seeds[10], N_WSH)).reshape((N_WSH, SEQS)).astype(jnp.int32)
    token_places = jax.vmap(lambda own: jax.random.permutation(own, GROUP_TOK))(jax.random.split(seeds[11], N_WSH)).reshape((N_WSH, GROUP_TOK)).astype(jnp.int32)
    expert_routes_keys = jax.random.split(jax.random.fold_in(seeds[12], 1), N_WSH * GROUP_TOK // TOK_DEV)
    expert_routes_turns = jax.random.permutation(jax.random.fold_in(seeds[12], 3), N_WSH * GROUP_TOK // TOK_DEV)
    expert_routes = jax.vmap(lambda own, number: shared_out(jax.random.fold_in(seeds[12], 2), own, number, TOK_DEV, EXPERTS, TOPK, CAP, 1))(expert_routes_keys, expert_routes_turns).reshape((N_WSH, GROUP_TOK, TOPK))
    cotangent = bell_draw(seeds[13], (N_WSH, GROUP_TOK, MODEL_SIZE), 1.0, 6.0, ((0, 4), (1, 8)))
    return {"layer_input": layer_input, "attention_gain": attention_gain, "query_weight": query_weight, "key_matrix": key_matrix, "value_matrix": value_matrix, "output_weight": output_weight, "expert_gain": expert_gain, "router_weight": router_weight, "expert_inner": expert_inner, "expert_outer": expert_outer, "document_lengths": document_lengths, "token_places": token_places, "expert_routes": expert_routes, "cotangent": cotangent}


@jax.custom_vjp
def lower_bound(v):
    return lax.optimization_barrier(v.astype(jnp.bfloat16)).astype(jnp.float32)

@jax.custom_vjp
def low_back(v):
    return v

def low_keep(v):
    return (lower_bound(v), None)

def low_pass(kept, grad):
    return (grad,)

def back_keep(v):
    return (v, None)

def back_low(kept, grad):
    return (lower_bound(grad),)
lower_bound.defvjp(low_keep, low_pass)
low_back.defvjp(back_keep, back_low)
EPS = 1e-05
THETA = 10000.0
MASK_FILL = -1e+30
HIGHEST = lax.Precision.HIGHEST

def exact_dot(operand, second):
    return jnp.dot(operand, second, precision=HIGHEST, preferred_element_type=jnp.float32)

def rms_inverse(matrix):
    return lax.rsqrt(lax.optimization_barrier(jnp.mean(matrix * matrix, axis=-1, keepdims=True)) + EPS)

def locate(lengths_row, places_row):
    segment_ends = jnp.cumsum(lengths_row)
    beyond = (places_row[:, None] >= segment_ends[None, :]).astype(jnp.int32)
    documents = lax.optimization_barrier(jnp.sum(beyond, axis=1))
    offsets = places_row - lax.optimization_barrier(jnp.sum(beyond * lengths_row[None, :], axis=1))
    return (documents, offsets)

def angles_for(offsets):
    halfway = HEAD_SIZE // 2
    frequency = THETA ** (-2.0 * jnp.arange(halfway, dtype=jnp.float32) / HEAD_SIZE)
    angles = offsets.astype(jnp.float32)[:, None] * frequency[None, :]
    return (jnp.cos(angles)[:, None, :], jnp.sin(angles)[:, None, :])

def apply_rotation(matrix, cosine_rows, sine_table):
    halfway = matrix.shape[-1] // 2
    former = matrix[..., :halfway]
    latter = matrix[..., halfway:]
    return jnp.concatenate([former * cosine_rows - latter * sine_table, latter * cosine_rows + former * sine_table], axis=-1)

def visible_mask(query_documents, query_places, key_documents, key_places):
    same_doc = (query_documents[:, None] == key_documents[None, :]) & (query_documents[:, None] < SEQS)
    causal = key_places[None, :] <= query_places[:, None]
    return same_doc & causal | (key_places[None, :] == query_places[:, None])

def attend(rows_of_queries, rows_of_keys, rows_of_values, visible):
    group_length = rows_of_queries.shape[0]
    grouped_queries = rows_of_queries.reshape(group_length, KEY_HEADS, QUERY_HEADS // KEY_HEADS, HEAD_SIZE).transpose(1, 2, 0, 3)

    def per_head(pieces):
        heads_of_queries, heads_of_keys, heads_of_values = pieces
        scores = low_back(jnp.einsum('rtd,kd->rtk', heads_of_queries, heads_of_keys, precision=HIGHEST) * HEAD_SIZE ** (-0.5))
        scores = jnp.where(visible[None], scores, MASK_FILL)
        attention_probs = jax.nn.softmax(scores, axis=-1)
        return jnp.einsum('rtk,kd->rtd', lower_bound(attention_probs), heads_of_values, precision=HIGHEST)
    outputs = lax.map(jax.checkpoint(per_head), (grouped_queries, rows_of_keys.transpose(1, 0, 2), rows_of_values.transpose(1, 0, 2)))
    return outputs.transpose(2, 0, 1, 3).reshape(group_length, QUERY_HEADS * HEAD_SIZE)

def expert_branch(normed, router_weight, expert_inner, expert_outer, route_table):
    logits = low_back(exact_dot(normed, router_weight))
    route_picks = (route_table[:, :, None] == jnp.arange(router_weight.shape[1], dtype=jnp.int32)[None, None, :]).astype(jnp.float32)
    chosen = lax.optimization_barrier(jnp.sum(route_picks * logits[:, None, :], axis=-1))
    gate_values = jax.nn.softmax(chosen, axis=-1)
    combine = lax.optimization_barrier(jnp.sum(route_picks * gate_values[:, :, None], axis=1))

    def add_expert(running_total, pieces):
        inner_matrix, outer_matrix, combine_column = pieces
        routed = low_back(normed)
        gate_up = low_back(exact_dot(routed, inner_matrix))
        hidden = lower_bound(jax.nn.silu(gate_up[:, :EXPERT_H]) * gate_up[:, EXPERT_H:])
        result = low_back(lower_bound(exact_dot(hidden, outer_matrix)))
        return (running_total + combine_column[:, None] * result, None)
    start_total = jnp.zeros(normed.shape, jnp.float32)
    mixture, leftover = lax.scan(jax.checkpoint(add_expert), start_total, (expert_inner, expert_outer, combine.T))
    return mixture

def forward(floats, document_lengths, token_places, expert_routes):
    layer_float, attention_gain, query_weight, key_matrix, value_matrix, output_weight, expert_gain, router_weight, expert_inner, expert_outer = floats

    def one_group(pieces):
        group_input, lengths_row, places_row = pieces
        documents, offsets = locate(lengths_row, places_row)
        cosine_rows, sine_table = angles_for(offsets)
        normed = lower_bound(group_input * rms_inverse(group_input) * attention_gain)
        query_pre = low_back(exact_dot(normed, query_weight))
        key_unrotated = low_back(exact_dot(normed, key_matrix))
        value_projected = low_back(exact_dot(normed, value_matrix))
        rows_of_queries = lower_bound(apply_rotation(query_pre.reshape(-1, QUERY_HEADS, HEAD_SIZE), cosine_rows, sine_table))
        rows_of_keys = lower_bound(apply_rotation(key_unrotated.reshape(-1, KEY_HEADS, HEAD_SIZE), cosine_rows, sine_table))
        rows_of_values = lower_bound(value_projected).reshape(-1, KEY_HEADS, HEAD_SIZE)
        visible = visible_mask(documents, places_row, documents, places_row)
        attended = attend(rows_of_queries, rows_of_keys, rows_of_values, visible)
        branch = low_back(exact_dot(low_back(lower_bound(attended)), output_weight))
        return group_input + branch
    residual = lax.map(jax.checkpoint(one_group), (layer_float, document_lengths, token_places))
    flat_residual = residual.reshape(-1, MODEL_SIZE)
    normed_two = lower_bound(flat_residual * rms_inverse(flat_residual) * expert_gain)
    mixture = expert_branch(normed_two, router_weight, expert_inner, expert_outer, expert_routes.reshape(-1, TOPK))
    return (flat_residual + mixture).reshape(residual.shape)

def reference(layer_input, attention_gain, query_weight, key_matrix, value_matrix, output_weight, expert_gain, router_weight, expert_inner, expert_outer, document_lengths, token_places, expert_routes, cotangent):
    floats = (layer_input.astype(jnp.float32), attention_gain.astype(jnp.float32), query_weight.astype(jnp.float32), key_matrix.astype(jnp.float32), value_matrix.astype(jnp.float32), output_weight.astype(jnp.float32), expert_gain.astype(jnp.float32), router_weight.astype(jnp.float32), expert_inner.astype(jnp.float32), expert_outer.astype(jnp.float32))

    def wrapped(values_tuple):
        return forward(values_tuple, document_lengths, token_places, expert_routes)
    output, pullback = jax.vjp(wrapped, floats)
    gradients, = pullback(cotangent.astype(jnp.float32))
    return (output.astype(jnp.bfloat16), gradients[0], gradients[1], gradients[2], gradients[3], gradients[4], gradients[5], gradients[6], gradients[7], gradients[8], gradients[9])
```

```python
import functools

import jax
import jax.numpy as jnp
from jax import lax
from jax.experimental import pallas as pl
from jax.experimental.pallas import tpu as pltpu
from jax.sharding import PartitionSpec as P

QUERY_HEADS = 24
KEY_HEADS = 8
HEAD_SIZE = 64
EXPERT_H = 512
TOPK = 8
SEQS = 4
GROUP = QUERY_HEADS // KEY_HEADS
PAIRS = KEY_HEADS // 2
PAIR_HEADS = 2 * GROUP
PAIR_WIDTH = 2 * HEAD_SIZE

EPS = 1e-05
THETA = 10000.0
MASK_FILL = -1e30
SCALE = HEAD_SIZE**-0.5
BF16 = jnp.bfloat16
F32 = jnp.float32


def dot(a, b):
    return jnp.dot(a, b, preferred_element_type=F32)


def dot_nt(a, b):
    return lax.dot_general(a, b, (((1,), (1,)), ((), ())), preferred_element_type=F32)


def dot_tn(a, b):
    return lax.dot_general(a, b, (((0,), (0,)), ((), ())), preferred_element_type=F32)


def rms_inverse(matrix):
    return lax.rsqrt(jnp.mean(matrix * matrix, axis=-1, keepdims=True) + EPS)


def locate(lengths_row, places_row):
    segment_ends = jnp.cumsum(lengths_row)
    beyond = (places_row[:, None] >= segment_ends[None, :]).astype(jnp.int32)
    documents = jnp.sum(beyond, axis=1)
    offsets = places_row - jnp.sum(beyond * lengths_row[None, :], axis=1)
    return (documents, offsets)


def angles_for(offsets):
    halfway = HEAD_SIZE // 2
    frequency = THETA ** (-2.0 * jnp.arange(halfway, dtype=F32) / HEAD_SIZE)
    angles = offsets.astype(F32)[:, None] * frequency[None, :]
    return (jnp.cos(angles)[:, None, :], jnp.sin(angles)[:, None, :])


def apply_rotation(matrix, cosine_rows, sine_table):
    halfway = matrix.shape[-1] // 2
    former = matrix[..., :halfway]
    latter = matrix[..., halfway:]
    return jnp.concatenate(
        [former * cosine_rows - latter * sine_table, latter * cosine_rows + former * sine_table],
        axis=-1,
    )


def reverse_rotation(matrix, cosine_rows, sine_table):
    return apply_rotation(matrix, cosine_rows, -sine_table)


def norm_backward(matrix, inverse, gains, gradients):
    scaled = gradients * gains
    gain_grad = jnp.sum(gradients * matrix * inverse, axis=0)
    input_back = inverse * scaled - matrix * inverse * inverse * inverse * jnp.mean(
        scaled * matrix, axis=-1, keepdims=True
    )
    return (gain_grad, input_back)


def spread_heads(rows):
    tokens = rows.shape[0]
    heads = rows.reshape(tokens, PAIRS, 2, GROUP, HEAD_SIZE).transpose(1, 2, 3, 4, 0)
    zero = jnp.zeros_like(heads[:, 0])
    low = jnp.concatenate([heads[:, 0], zero], axis=2)
    high = jnp.concatenate([zero, heads[:, 1]], axis=2)
    return jnp.stack([low, high], axis=1).reshape(PAIRS, PAIR_HEADS, PAIR_WIDTH, tokens)


def gather_heads(spread):
    tokens = spread.shape[-1]
    split = spread.reshape(PAIRS, 2, GROUP, 2, HEAD_SIZE, tokens)
    heads = jnp.stack([split[:, 0, :, 0], split[:, 1, :, 1]], axis=1)
    return heads.transpose(4, 0, 1, 2, 3).reshape(tokens, QUERY_HEADS * HEAD_SIZE)


def fill_bias(bias_ref, kdoc_ref, kplace_ref, qdoc_ref, qplace_ref):
    kdoc, kplace = kdoc_ref[...], kplace_ref[...]
    qdoc, qplace = qdoc_ref[...], qplace_ref[...]
    seen = (kdoc == qdoc) & (qdoc < SEQS) & (kplace <= qplace) | (kplace == qplace)
    bias_ref[...] = jnp.where(seen, 0.0, MASK_FILL)


def attend_kernel(
    q_ref, k_ref, v_ref, kdoc_ref, kplace_ref, qdoc_ref, qplace_ref, o_ref, lse_ref, bias, vt
):
    pair, head = pl.program_id(0), pl.program_id(1)

    @pl.when((pair == 0) & (head == 0))
    def _():
        fill_bias(bias, kdoc_ref, kplace_ref, qdoc_ref, qplace_ref)

    @pl.when(head == 0)
    def _():
        vt[...] = v_ref[...].T

    scores = dot(k_ref[...], q_ref[0, 0]) + bias[...]
    top = jnp.max(scores, axis=0, keepdims=True)
    weights = jnp.exp(scores - top)
    total = jnp.sum(weights, axis=0, keepdims=True)
    o_ref[0, 0] = dot(vt[...], weights.astype(BF16)) / total
    lse_ref[0, 0] = top + jnp.log(total)


def attend_back_kernel(
    q_ref,
    qt_ref,
    g_ref,
    gt_ref,
    k_ref,
    v_ref,
    lse_ref,
    delta_ref,
    kdoc_ref,
    kplace_ref,
    qdoc_ref,
    qplace_ref,
    dq_ref,
    dk_ref,
    dv_ref,
    bias,
    kt,
    dk_sum,
    dv_sum,
):
    pair, head = pl.program_id(0), pl.program_id(1)

    @pl.when((pair == 0) & (head == 0))
    def _():
        fill_bias(bias, kdoc_ref, kplace_ref, qdoc_ref, qplace_ref)

    @pl.when(head == 0)
    def _():
        kt[...] = k_ref[...].T
        dk_sum[...] = jnp.zeros_like(dk_sum)
        dv_sum[...] = jnp.zeros_like(dv_sum)

    scores = dot(k_ref[...], q_ref[0, 0]) + bias[...]
    probs = jnp.exp(scores - lse_ref[0, 0])
    prob_grad = dot(v_ref[...], g_ref[0, 0])
    score_grad = (probs * (prob_grad - delta_ref[0, 0])).astype(BF16)
    dv_sum[...] += dot(probs.astype(BF16), gt_ref[0, 0])
    dk_sum[...] += dot(score_grad, qt_ref[0, 0])
    dq_ref[0, 0] = dot(kt[...], score_grad)

    @pl.when(head == PAIR_HEADS - 1)
    def _():
        dk_ref[...] = dk_sum[...].astype(BF16)
        dv_ref[...] = dv_sum[...].astype(BF16)


def whole(shape):
    return pl.BlockSpec(shape, lambda *_: (0,) * len(shape))


def attention_specs(tokens, rows):
    head = pl.BlockSpec((1, 1, PAIR_WIDTH, tokens), lambda p, h: (p, h, 0, 0))
    head_t = pl.BlockSpec((1, 1, tokens, PAIR_WIDTH), lambda p, h: (p, h, 0, 0))
    line = pl.BlockSpec((1, 1, 1, tokens), lambda p, h: (p, h, 0, 0))
    keys = pl.BlockSpec((rows, PAIR_WIDTH), lambda p, h: (0, p))
    marks = [whole((rows, 1)), whole((rows, 1)), whole((1, tokens)), whole((1, tokens))]
    return head, head_t, line, keys, marks


def attend(queries, keys, values, marks):
    tokens, rows = queries.shape[-1], keys.shape[0]
    head, _, line, key_spec, mark_specs = attention_specs(tokens, rows)
    return pl.pallas_call(
        attend_kernel,
        grid=(PAIRS, PAIR_HEADS),
        in_specs=[head, key_spec, key_spec] + mark_specs,
        out_specs=[head, line],
        out_shape=[
            jax.ShapeDtypeStruct((PAIRS, PAIR_HEADS, PAIR_WIDTH, tokens), F32),
            jax.ShapeDtypeStruct((PAIRS, PAIR_HEADS, 1, tokens), F32),
        ],
        scratch_shapes=[pltpu.VMEM((rows, tokens), F32), pltpu.VMEM((PAIR_WIDTH, rows), BF16)],
        cost_estimate=pl.CostEstimate(
            flops=4 * QUERY_HEADS * tokens * rows * PAIR_WIDTH,
            bytes_accessed=16 << 20,
            transcendentals=QUERY_HEADS * tokens * rows,
        ),
        name="attend",
    )(queries, keys, values, *marks)


def attend_back(queries, queries_t, grads, grads_t, keys, values, lse, delta, marks):
    tokens, rows = queries.shape[-1], keys.shape[0]
    head, head_t, line, key_spec, mark_specs = attention_specs(tokens, rows)
    return pl.pallas_call(
        attend_back_kernel,
        grid=(PAIRS, PAIR_HEADS),
        in_specs=[head, head_t, head, head_t, key_spec, key_spec, line, line] + mark_specs,
        out_specs=[head, key_spec, key_spec],
        out_shape=[
            jax.ShapeDtypeStruct((PAIRS, PAIR_HEADS, PAIR_WIDTH, tokens), F32),
            jax.ShapeDtypeStruct(keys.shape, BF16),
            jax.ShapeDtypeStruct(keys.shape, BF16),
        ],
        scratch_shapes=[
            pltpu.VMEM((rows, tokens), F32),
            pltpu.VMEM((PAIR_WIDTH, rows), BF16),
            pltpu.VMEM((rows, PAIR_WIDTH), F32),
            pltpu.VMEM((rows, PAIR_WIDTH), F32),
        ],
        cost_estimate=pl.CostEstimate(
            flops=10 * QUERY_HEADS * tokens * rows * PAIR_WIDTH,
            bytes_accessed=24 << 20,
            transcendentals=QUERY_HEADS * tokens * rows,
        ),
        name="attend_back",
    )(queries, queries_t, grads, grads_t, keys, values, lse, delta, *marks)


def expert_kernel(
    x_ref, g_ref, w_ref, wi_ref, wo_ref, mix_ref, back_ref, gate_ref, dwi_ref, dwo_ref, dwi, dwo, mid, rows
):
    step = pl.program_id(0)
    count, width = wi_ref.shape[0], wi_ref.shape[1]

    @pl.when(step == 0)
    def _():
        dwi[...] = jnp.zeros_like(dwi)
        dwo[...] = jnp.zeros_like(dwo)

    grad = g_ref[...]
    for e in range(count):
        gate_up = dot(x_ref[...], wi_ref[e])
        gate, up = gate_up[:, :EXPERT_H], gate_up[:, EXPERT_H:]
        sigmoid = 1.0 / (1.0 + jnp.exp(-gate))
        silu = gate * sigmoid
        hidden = (silu * up).astype(BF16).astype(F32)
        weight = w_ref[:, e : e + 1]
        inward = dot_nt(grad, wo_ref[e])
        gate_ref[:, e : e + 1] = jnp.sum(hidden * inward, axis=1, keepdims=True)
        weighted = (weight * hidden).astype(BF16)
        hidden_grad = weight * inward
        mid[:, e * EXPERT_H : (e + 1) * EXPERT_H] = weighted
        at = 2 * e * EXPERT_H
        rows[:, at : at + EXPERT_H] = (
            hidden_grad * up * sigmoid * (1.0 + gate * (1.0 - sigmoid))
        ).astype(BF16)
        rows[:, at + EXPERT_H : at + 2 * EXPERT_H] = (hidden_grad * silu).astype(BF16)
        dwo[e] += dot_tn(weighted, grad)
    tile = 256
    for e in range(count):
        inner = rows[:, 2 * e * EXPERT_H : 2 * (e + 1) * EXPERT_H]

        @pl.loop(0, width // tile)
        def _(t):
            at = pl.multiple_of(t * tile, tile)
            dwi[e, pl.ds(at, tile), :] += dot_tn(x_ref[:, pl.ds(at, tile)], inner)

    @pl.loop(0, width // tile)
    def _(t):
        at = pl.multiple_of(t * tile, tile)
        mixed, back = 0.0, 0.0
        for e in range(count):
            mixed += dot(mid[:, e * EXPERT_H : (e + 1) * EXPERT_H], wo_ref[e, :, pl.ds(at, tile)])
            back += dot_nt(
                rows[:, 2 * e * EXPERT_H : 2 * (e + 1) * EXPERT_H], wi_ref[e, pl.ds(at, tile), :]
            )
        mix_ref[:, pl.ds(at, tile)] = mixed.astype(BF16)
        back_ref[:, pl.ds(at, tile)] = back.astype(BF16)

    @pl.when(step == pl.num_programs(0) - 1)
    def _():
        dwi_ref[...] = dwi[...].astype(BF16)
        dwo_ref[...] = dwo[...].astype(BF16)


def experts_pass(tokens, grads, weights, inner, outer):
    rows, width = tokens.shape
    block = 256
    row_spec = pl.BlockSpec((block, width), lambda i: (i, 0))
    count = inner.shape[0]
    gate_spec = pl.BlockSpec((block, count), lambda i: (i, 0))
    once = pl.Buffered(1)
    inner_spec = pl.BlockSpec(inner.shape, lambda i: (0, 0, 0), pipeline_mode=once)
    outer_spec = pl.BlockSpec(outer.shape, lambda i: (0, 0, 0), pipeline_mode=once)
    return pl.pallas_call(
        expert_kernel,
        grid=(rows // block,),
        in_specs=[row_spec, row_spec, gate_spec, inner_spec, outer_spec],
        out_specs=[row_spec, row_spec, gate_spec, inner_spec, outer_spec],
        out_shape=[
            jax.ShapeDtypeStruct((rows, width), BF16),
            jax.ShapeDtypeStruct((rows, width), BF16),
            jax.ShapeDtypeStruct((rows, count), F32),
            jax.ShapeDtypeStruct(inner.shape, BF16),
            jax.ShapeDtypeStruct(outer.shape, BF16),
        ],
        scratch_shapes=[
            pltpu.VMEM(inner.shape, F32),
            pltpu.VMEM(outer.shape, F32),
            pltpu.VMEM((block, count * EXPERT_H), BF16),
            pltpu.VMEM((block, 2 * count * EXPERT_H), BF16),
        ],
        compiler_params=pltpu.CompilerParams(vmem_limit_bytes=60 << 20),
        cost_estimate=pl.CostEstimate(
            flops=18 * count * rows * width * EXPERT_H,
            bytes_accessed=48 << 20,
            transcendentals=rows * count * EXPERT_H,
        ),
        name="experts",
    )(tokens, grads, weights, inner, outer)


MESH = pl.DeviceIdType.MESH
SLOW = 4
CHUNKS = 2


def ring_position(index, size):
    fast = size // SLOW
    row, column = lax.div(index, fast), lax.rem(index, fast)
    back = SLOW - 1 - row
    odd = lax.rem(back, 2)
    along = (column - 1) * (1 - odd) + (fast - 1 - column) * odd
    away = lax.div(column + fast - 2, fast - 1)
    return (1 - away) * row + away * (SLOW + back * (fast - 1) + along)


def ring_index(position, size):
    fast = size // SLOW
    away = lax.div(lax.div(position, SLOW) + fast - 2, fast - 1)
    rest = away * (position - SLOW)
    back, step = lax.div(rest, fast - 1), lax.rem(rest, fast - 1)
    odd = lax.rem(back, 2)
    column = (1 + step) * (1 - odd) + (fast - 1 - step) * odd
    return (1 - away) * position * fast + away * ((SLOW - 1 - back) * fast + column)


class Ring:
    def __init__(self, size):
        self.size, self.steps = size, size // 2
        self.me = lax.axis_index("ctx")
        self.place = ring_position(self.me, size)

    def at(self, shift):
        return ring_index(lax.rem(self.place + shift + self.size, self.size), self.size)

    def toward(self, direction, distance):
        return self.at(distance if direction == 0 else -distance)

    def device(self, direction):
        return (self.toward(direction, 1), lax.axis_index("wsh"))

    def meet(self):
        barrier = pltpu.get_barrier_semaphore()
        for direction in range(2):
            pl.semaphore_signal(
                barrier, inc=1, device_id=self.device(direction), device_id_type=MESH
            )
        pl.semaphore_wait(barrier, 2)

    def chunks(self, direction, last):
        if not last:
            return range(CHUNKS)
        half = CHUNKS // 2
        return range(half) if direction == 0 else range(half, CHUNKS)


def rows_at(block, rows, chunk):
    part = rows // CHUNKS
    return pl.ds(pl.multiple_of(block * rows + chunk * part, part), part)


def ring_gather_kernel(size, count, *refs):
    locals_, outs = refs[:count], refs[count : 2 * count]
    send, recv, own = refs[2 * count :]
    ring = Ring(size)
    ring.meet()

    def copy(k, direction, step, chunk, block):
        rows = locals_[k].shape[0]
        source = (
            locals_[k].at[rows_at(0, rows, chunk)]
            if step == 0
            else outs[k].at[rows_at(block, rows, chunk)]
        )
        return pltpu.make_async_remote_copy(
            src_ref=source,
            dst_ref=outs[k].at[rows_at(block, rows, chunk)],
            send_sem=send.at[k, direction, step, chunk],
            recv_sem=recv.at[k, direction, step, chunk],
            device_id=ring.device(direction),
            device_id_type=MESH,
        )

    started = []
    kept = []
    for step in range(ring.steps):
        for chunk in range(CHUNKS):
            for direction in range(2):
                if step > 0:
                    for k in range(count):
                        block = ring.toward(1 - direction, step)
                        copy(k, direction, step - 1, chunk, block).wait_recv()
                if chunk in ring.chunks(direction, step == ring.steps - 1):
                    for k in range(count):
                        moved = copy(k, direction, step, chunk, ring.toward(1 - direction, step))
                        moved.start()
                        started.append(moved)
        if step == 0:
            for k in range(count):
                rows = locals_[k].shape[0]
                place = pl.ds(pl.multiple_of(ring.me * rows, rows), rows)
                kept.append(pltpu.make_async_copy(locals_[k], outs[k].at[place], own.at[k]))
                kept[-1].start()
    last = ring.steps - 1
    for direction in range(2):
        for chunk in ring.chunks(direction, True):
            for k in range(count):
                copy(k, direction, last, chunk, ring.toward(1 - direction, last + 1)).wait_recv()
    for moved in started:
        moved.wait_send()
    for moved in kept:
        moved.wait()


def ring_gather(arrays, size, identity, name):
    count = len(arrays)
    sems = pltpu.SemaphoreType.DMA((count, 2, size // 2, CHUNKS))
    return pl.pallas_call(
        functools.partial(ring_gather_kernel, size, count),
        in_specs=[pl.BlockSpec(memory_space=pltpu.VMEM)] * count,
        out_specs=[pl.BlockSpec(memory_space=pl.ANY)] * count,
        out_shape=[
            jax.ShapeDtypeStruct((size * a.shape[0],) + a.shape[1:], a.dtype) for a in arrays
        ],
        scratch_shapes=[sems, sems, pltpu.SemaphoreType.DMA((count,))],
        compiler_params=pltpu.CompilerParams(collective_id=identity, has_side_effects=True),
        cost_estimate=pl.CostEstimate(flops=0, bytes_accessed=100 << 20, transcendentals=0),
        name=name,
    )(*arrays)


def ring_scatter_kernel(size, count, *refs):
    parts, outs = refs[:count], refs[count : 2 * count]
    stages, lands = refs[2 * count : 3 * count], refs[3 * count : 4 * count]
    send, recv = refs[4 * count :]
    ring = Ring(size)
    ring.meet()

    def copy(k, direction, step, chunk):
        rows = outs[k].shape[0]
        if step == 0:
            source = parts[k].at[rows_at(ring.toward(direction, ring.steps), rows, chunk)]
        else:
            source = stages[k].at[direction, step - 1, rows_at(0, rows, chunk)]
        return pltpu.make_async_remote_copy(
            src_ref=source,
            dst_ref=lands[k].at[direction, step, rows_at(0, rows, chunk)],
            send_sem=send.at[k, direction, step, chunk],
            recv_sem=recv.at[k, direction, step, chunk],
            device_id=ring.device(direction),
            device_id_type=MESH,
        )

    started = []
    for step in range(ring.steps):
        for chunk in range(CHUNKS):
            for direction in range(2):
                for k in range(count):
                    rows = outs[k].shape[0]
                    if step == 0:
                        if chunk not in ring.chunks(direction, True):
                            continue
                    else:
                        here = rows_at(0, rows, chunk)
                        dest = ring.toward(direction, ring.steps - step)
                        total = parts[k][rows_at(dest, rows, chunk)]
                        if step > 1 or chunk in ring.chunks(direction, True):
                            copy(k, direction, step - 1, chunk).wait_recv()
                            landed = lands[k][direction, step - 1, here]
                            total = (total.astype(F32) + landed.astype(F32)).astype(total.dtype)
                        stages[k][direction, step - 1, here] = total
                    moved = copy(k, direction, step, chunk)
                    moved.start()
                    started.append(moved)
    last = ring.steps - 1
    for chunk in range(CHUNKS):
        for k in range(count):
            rows = outs[k].shape[0]
            here = rows_at(0, rows, chunk)
            total = parts[k][rows_at(ring.me, rows, chunk)].astype(F32)
            for direction in range(2):
                copy(k, direction, last, chunk).wait_recv()
                total += lands[k][direction, last, here].astype(F32)
            outs[k][here] = total
    for moved in started:
        moved.wait_send()


def ring_scatter(arrays, size, identity, name):
    count, steps = len(arrays), size // 2
    sems = pltpu.SemaphoreType.DMA((count, 2, steps, CHUNKS))
    blocks = [(a.shape[0] // size,) + a.shape[1:] for a in arrays]
    vmem = pl.BlockSpec(memory_space=pltpu.VMEM)
    return pl.pallas_call(
        functools.partial(ring_scatter_kernel, size, count),
        in_specs=[vmem] * count,
        out_specs=[vmem] * count,
        out_shape=[jax.ShapeDtypeStruct(b, F32) for b in blocks],
        scratch_shapes=[
            pltpu.VMEM((2, steps - 1) + b, a.dtype) for a, b in zip(arrays, blocks)
        ]
        + [pltpu.VMEM((2, steps) + b, a.dtype) for a, b in zip(arrays, blocks)]
        + [sems, sems],
        compiler_params=pltpu.CompilerParams(
            collective_id=identity, has_side_effects=True, vmem_limit_bytes=48 << 20
        ),
        cost_estimate=pl.CostEstimate(flops=0, bytes_accessed=100 << 20, transcendentals=0),
        name=name,
    )(*arrays)


def on_device(
    layer_input,
    attention_gain,
    query_weight,
    key_matrix,
    value_matrix,
    output_weight,
    expert_gain,
    router_weight,
    expert_inner,
    expert_outer,
    document_lengths,
    token_places,
    expert_routes,
    cotangent,
):
    group_devices = lax.axis_size("ctx")
    ctx_index = lax.axis_index("ctx")
    token_rows = layer_input.shape[1]
    experts = router_weight.shape[1]
    own_experts = expert_inner.shape[0]
    key_value_width = KEY_HEADS * HEAD_SIZE

    def gather(shard, axis=0):
        return lax.all_gather(shard, "wsh", axis=axis, tiled=True)

    small = gather(
        jnp.concatenate([attention_gain[:, None], expert_gain[:, None], router_weight], axis=1)
    )
    gain_one, gain_two = small[:, 0].astype(F32), small[:, 1].astype(F32)
    whole_router = small[:, 2:]
    whole_key = gather(key_matrix)
    whole_value = gather(value_matrix)
    whole_query = gather(query_weight)
    whole_output = gather(output_weight)
    whole_inner = gather(expert_inner, 1)
    whole_outer = gather(expert_outer, 1)
    all_grads = lax.all_gather(cotangent[0], "ctx", axis=0, tiled=True)

    places_all = token_places[0]
    key_documents, key_offsets = locate(document_lengths[0], places_all)
    first_row = ctx_index * token_rows
    query_places = lax.dynamic_slice_in_dim(places_all, first_row, token_rows)
    query_documents = lax.dynamic_slice_in_dim(key_documents, first_row, token_rows)
    query_offsets = lax.dynamic_slice_in_dim(key_offsets, first_row, token_rows)
    marks = (
        key_documents[:, None],
        places_all[:, None],
        query_documents[None, :],
        query_places[None, :],
    )
    cosine_rows, sine_table = angles_for(query_offsets)

    inputs_f = layer_input[0].astype(F32)
    inverse_one = rms_inverse(inputs_f)
    normed_one = (inputs_f * inverse_one * gain_one).astype(BF16)
    key_pre = dot(normed_one, whole_key)
    keys = (
        apply_rotation(key_pre.reshape(token_rows, KEY_HEADS, HEAD_SIZE), cosine_rows, sine_table)
        .astype(BF16)
        .reshape(token_rows, key_value_width)
    )
    values = dot(normed_one, whole_value).astype(BF16)
    all_keys, all_values = ring_gather([keys, values], group_devices, 1, "gather_keys")
    query_pre = dot(normed_one, whole_query)
    queries = (
        apply_rotation(
            query_pre.reshape(token_rows, QUERY_HEADS, HEAD_SIZE), cosine_rows, sine_table
        ).astype(BF16)
        * SCALE
    ).reshape(token_rows, QUERY_HEADS * HEAD_SIZE)
    spread_queries = spread_heads(queries)
    spread_attended, lse = attend(spread_queries, all_keys, all_values, marks)
    attended_f = gather_heads(spread_attended)
    attended = attended_f.astype(BF16)
    residual = inputs_f + dot(attended, whole_output)
    inverse_two = rms_inverse(residual)
    normed_two = (residual * inverse_two * gain_two).astype(BF16)
    logits = dot(normed_two, whole_router)
    expert_ids = jnp.arange(experts, dtype=jnp.int32)
    routed = jnp.any(expert_routes[0][:, :, None] == expert_ids[None, None, :], axis=1)
    gates = jax.nn.softmax(jnp.where(routed, logits, -jnp.inf), axis=-1)

    all_tokens, all_gates = ring_gather([normed_two, gates.T], group_devices, 2, "gather_tokens")
    own_gates = (
        lax.dynamic_slice_in_dim(
            all_gates.reshape(group_devices, experts, token_rows),
            ctx_index * own_experts,
            own_experts,
            axis=1,
        )
        .transpose(0, 2, 1)
        .reshape(group_devices * token_rows, own_experts)
    )
    mixed, back_rows, own_gate_grad, inner_grad, outer_grad = experts_pass(
        all_tokens, all_grads, own_gates, whole_inner, whole_outer
    )
    placed = lax.dynamic_update_slice_in_dim(
        jnp.zeros((group_devices, experts, token_rows), F32),
        own_gate_grad.reshape(group_devices, token_rows, own_experts).transpose(0, 2, 1),
        ctx_index * own_experts,
        axis=1,
    ).reshape(group_devices * experts, token_rows)
    back_sum, gate_grad = ring_scatter([back_rows, placed], group_devices, 3, "scatter_rows")
    gate_grad = gate_grad.T
    mixture = lax.psum_scatter(mixed, "ctx", scatter_dimension=0, tiled=True)
    layer_output = (residual + mixture.astype(F32)).astype(BF16)

    out_grad = cotangent[0].astype(F32)
    logit_grad = (
        gates * (gate_grad - jnp.sum(gates * gate_grad, axis=-1, keepdims=True))
    ).astype(BF16)
    router_grad = dot_tn(normed_two, logit_grad)
    normed_two_grad = dot_nt(logit_grad, whole_router) + back_sum
    gain_two_grad, residual_back = norm_backward(residual, inverse_two, gain_two, normed_two_grad)
    residual_grad = out_grad + residual_back
    branch_grad = residual_grad.astype(BF16)
    output_grad = dot_tn(attended, branch_grad)
    attended_grad = dot_nt(branch_grad, whole_output).astype(BF16)
    delta = jnp.sum(
        (attended_grad.astype(F32) * attended_f).reshape(token_rows, QUERY_HEADS, HEAD_SIZE), axis=-1
    ).T.reshape(PAIRS, PAIR_HEADS, 1, token_rows)
    spread_grads = spread_heads(attended_grad)
    spread_query_grad, key_part, value_part = attend_back(
        spread_queries,
        spread_queries.transpose(0, 1, 3, 2),
        spread_grads,
        spread_grads.transpose(0, 1, 3, 2),
        all_keys,
        all_values,
        lse,
        delta,
        marks,
    )
    key_grad, value_grad = ring_scatter([key_part, value_part], group_devices, 4, "scatter_keys")
    value_grad = value_grad.astype(BF16)
    query_pre_grad = (
        reverse_rotation(
            (gather_heads(spread_query_grad) * SCALE).reshape(token_rows, QUERY_HEADS, HEAD_SIZE),
            cosine_rows,
            sine_table,
        )
        .reshape(token_rows, QUERY_HEADS * HEAD_SIZE)
        .astype(BF16)
    )
    key_pre_grad = (
        reverse_rotation(
            key_grad.reshape(token_rows, KEY_HEADS, HEAD_SIZE), cosine_rows, sine_table
        )
        .reshape(token_rows, key_value_width)
        .astype(BF16)
    )
    query_weight_grad = dot_tn(normed_one, query_pre_grad)
    key_weight_grad = dot_tn(normed_one, key_pre_grad)
    value_weight_grad = dot_tn(normed_one, value_grad)
    normed_one_grad = (
        dot_nt(query_pre_grad, whole_query)
        + dot_nt(key_pre_grad, whole_key)
        + dot_nt(value_grad, whole_value)
    )
    gain_one_grad, input_back = norm_backward(inputs_f, inverse_one, gain_one, normed_one_grad)
    input_grad = residual_grad + input_back

    def scatter(grad, dim=0):
        return lax.psum_scatter(grad.astype(BF16), "wsh", scatter_dimension=dim, tiled=True)

    def reduce(grad):
        return lax.psum(scatter(grad), "ctx").astype(F32)

    inner_out = scatter(inner_grad, 1).astype(F32)
    outer_out = scatter(outer_grad, 1).astype(F32)
    output_out = reduce(output_grad)
    query_out = reduce(query_weight_grad)
    key_value_out = reduce(jnp.concatenate([key_weight_grad, value_weight_grad], axis=1))
    small_out = reduce(
        jnp.concatenate([gain_one_grad[:, None], gain_two_grad[:, None], router_grad], axis=1)
    )
    return (
        layer_output[None],
        input_grad[None],
        small_out[:, 0],
        query_out,
        key_value_out[:, :key_value_width],
        key_value_out[:, key_value_width:],
        output_out,
        small_out[:, 1],
        small_out[:, 2:],
        inner_out,
        outer_out,
    )


def solution(mesh):
    tokens = P("wsh", "ctx", None)
    shard, expert = P("wsh", None), P("ctx", "wsh", None)
    return jax.shard_map(
        on_device,
        mesh=mesh,
        in_specs=(
            tokens,
            P("wsh"),
            shard,
            shard,
            shard,
            shard,
            P("wsh"),
            shard,
            expert,
            expert,
            shard,
            shard,
            tokens,
            tokens,
        ),
        out_specs=(
            tokens,
            tokens,
            P("wsh"),
            shard,
            shard,
            shard,
            shard,
            P("wsh"),
            shard,
            expert,
            expert,
        ),
        check_vma=False,
    )
```

```python
import functools

import jax
import jax.numpy as jnp
from jax import lax
from jax.experimental import pallas as pl
from jax.experimental.pallas import tpu as pltpu
from jax.sharding import PartitionSpec as P

QUERY_HEADS = 24
KEY_HEADS = 8
HEAD_SIZE = 64
EXPERT_H = 512
TOPK = 8
SEQS = 4
GROUP = QUERY_HEADS // KEY_HEADS
PAIRS = KEY_HEADS // 2
PAIR_HEADS = 2 * GROUP
PAIR_WIDTH = 2 * HEAD_SIZE

EPS = 1e-05
THETA = 10000.0
MASK_FILL = -1e30
SCALE = HEAD_SIZE**-0.5
BF16 = jnp.bfloat16
F32 = jnp.float32


def dot(a, b):
    return jnp.dot(a, b, preferred_element_type=F32)


def dot_nt(a, b):
    return lax.dot_general(a, b, (((1,), (1,)), ((), ())), preferred_element_type=F32)


def dot_tn(a, b):
    return lax.dot_general(a, b, (((0,), (0,)), ((), ())), preferred_element_type=F32)


def rms_inverse(matrix):
    return lax.rsqrt(jnp.mean(matrix * matrix, axis=-1, keepdims=True) + EPS)


def locate(lengths_row, places_row):
    segment_ends = jnp.cumsum(lengths_row)
    beyond = (places_row[:, None] >= segment_ends[None, :]).astype(jnp.int32)
    documents = jnp.sum(beyond, axis=1)
    offsets = places_row - jnp.sum(beyond * lengths_row[None, :], axis=1)
    return (documents, offsets)


def angles_for(offsets):
    halfway = HEAD_SIZE // 2
    frequency = THETA ** (-2.0 * jnp.arange(halfway, dtype=F32) / HEAD_SIZE)
    angles = offsets.astype(F32)[:, None] * frequency[None, :]
    return (jnp.cos(angles)[:, None, :], jnp.sin(angles)[:, None, :])


def apply_rotation(matrix, cosine_rows, sine_table):
    halfway = matrix.shape[-1] // 2
    former = matrix[..., :halfway]
    latter = matrix[..., halfway:]
    return jnp.concatenate(
        [former * cosine_rows - latter * sine_table, latter * cosine_rows + former * sine_table],
        axis=-1,
    )


def reverse_rotation(matrix, cosine_rows, sine_table):
    return apply_rotation(matrix, cosine_rows, -sine_table)


def norm_backward(matrix, inverse, gains, gradients):
    scaled = gradients * gains
    gain_grad = jnp.sum(gradients * matrix * inverse, axis=0)
    input_back = inverse * scaled - matrix * inverse * inverse * inverse * jnp.mean(
        scaled * matrix, axis=-1, keepdims=True
    )
    return (gain_grad, input_back)


def spread_heads(rows):
    tokens = rows.shape[0]
    heads = rows.reshape(tokens, PAIRS, 2, GROUP, HEAD_SIZE).transpose(1, 2, 3, 4, 0)
    zero = jnp.zeros_like(heads[:, 0])
    low = jnp.concatenate([heads[:, 0], zero], axis=2)
    high = jnp.concatenate([zero, heads[:, 1]], axis=2)
    return jnp.stack([low, high], axis=1).reshape(PAIRS, PAIR_HEADS, PAIR_WIDTH, tokens)


def gather_heads(spread):
    tokens = spread.shape[-1]
    split = spread.reshape(PAIRS, 2, GROUP, 2, HEAD_SIZE, tokens)
    heads = jnp.stack([split[:, 0, :, 0], split[:, 1, :, 1]], axis=1)
    return heads.transpose(4, 0, 1, 2, 3).reshape(tokens, QUERY_HEADS * HEAD_SIZE)


def fill_bias(bias_ref, kdoc_ref, kplace_ref, qdoc_ref, qplace_ref):
    kdoc, kplace = kdoc_ref[...], kplace_ref[...]
    qdoc, qplace = qdoc_ref[...], qplace_ref[...]
    seen = (kdoc == qdoc) & (qdoc < SEQS) & (kplace <= qplace) | (kplace == qplace)
    bias_ref[...] = jnp.where(seen, 0.0, MASK_FILL)


def attend_kernel(
    q_ref, k_ref, v_ref, kdoc_ref, kplace_ref, qdoc_ref, qplace_ref, o_ref, lse_ref, bias, vt
):
    pair, head = pl.program_id(0), pl.program_id(1)

    @pl.when((pair == 0) & (head == 0))
    def _():
        fill_bias(bias, kdoc_ref, kplace_ref, qdoc_ref, qplace_ref)

    @pl.when(head == 0)
    def _():
        vt[...] = v_ref[...].T

    scores = dot(k_ref[...], q_ref[0, 0]) + bias[...]
    top = jnp.max(scores, axis=0, keepdims=True)
    weights = jnp.exp(scores - top)
    total = jnp.sum(weights, axis=0, keepdims=True)
    o_ref[0, 0] = dot(vt[...], weights.astype(BF16)) / total
    lse_ref[0, 0] = top + jnp.log(total)


def attend_back_kernel(
    q_ref,
    qt_ref,
    g_ref,
    gt_ref,
    k_ref,
    v_ref,
    lse_ref,
    delta_ref,
    kdoc_ref,
    kplace_ref,
    qdoc_ref,
    qplace_ref,
    dq_ref,
    dk_ref,
    dv_ref,
    bias,
    kt,
    dk_sum,
    dv_sum,
):
    pair, head = pl.program_id(0), pl.program_id(1)

    @pl.when((pair == 0) & (head == 0))
    def _():
        fill_bias(bias, kdoc_ref, kplace_ref, qdoc_ref, qplace_ref)

    @pl.when(head == 0)
    def _():
        kt[...] = k_ref[...].T
        dk_sum[...] = jnp.zeros_like(dk_sum)
        dv_sum[...] = jnp.zeros_like(dv_sum)

    scores = dot(k_ref[...], q_ref[0, 0]) + bias[...]
    probs = jnp.exp(scores - lse_ref[0, 0])
    prob_grad = dot(v_ref[...], g_ref[0, 0])
    score_grad = (probs * (prob_grad - delta_ref[0, 0])).astype(BF16)
    dv_sum[...] += dot(probs.astype(BF16), gt_ref[0, 0])
    dk_sum[...] += dot(score_grad, qt_ref[0, 0])
    dq_ref[0, 0] = dot(kt[...], score_grad)

    @pl.when(head == PAIR_HEADS - 1)
    def _():
        dk_ref[...] = dk_sum[...].astype(BF16)
        dv_ref[...] = dv_sum[...].astype(BF16)


def whole(shape):
    return pl.BlockSpec(shape, lambda *_: (0,) * len(shape))


def attention_specs(tokens, rows):
    head = pl.BlockSpec((1, 1, PAIR_WIDTH, tokens), lambda p, h: (p, h, 0, 0))
    head_t = pl.BlockSpec((1, 1, tokens, PAIR_WIDTH), lambda p, h: (p, h, 0, 0))
    line = pl.BlockSpec((1, 1, 1, tokens), lambda p, h: (p, h, 0, 0))
    keys = pl.BlockSpec((rows, PAIR_WIDTH), lambda p, h: (0, p))
    marks = [whole((rows, 1)), whole((rows, 1)), whole((1, tokens)), whole((1, tokens))]
    return head, head_t, line, keys, marks


def attend(queries, keys, values, marks):
    tokens, rows = queries.shape[-1], keys.shape[0]
    head, _, line, key_spec, mark_specs = attention_specs(tokens, rows)
    return pl.pallas_call(
        attend_kernel,
        grid=(PAIRS, PAIR_HEADS),
        in_specs=[head, key_spec, key_spec] + mark_specs,
        out_specs=[head, line],
        out_shape=[
            jax.ShapeDtypeStruct((PAIRS, PAIR_HEADS, PAIR_WIDTH, tokens), F32),
            jax.ShapeDtypeStruct((PAIRS, PAIR_HEADS, 1, tokens), F32),
        ],
        scratch_shapes=[pltpu.VMEM((rows, tokens), F32), pltpu.VMEM((PAIR_WIDTH, rows), BF16)],
        cost_estimate=pl.CostEstimate(
            flops=4 * QUERY_HEADS * tokens * rows * PAIR_WIDTH,
            bytes_accessed=16 << 20,
            transcendentals=QUERY_HEADS * tokens * rows,
        ),
        name="attend",
    )(queries, keys, values, *marks)


def attend_back(queries, queries_t, grads, grads_t, keys, values, lse, delta, marks):
    tokens, rows = queries.shape[-1], keys.shape[0]
    head, head_t, line, key_spec, mark_specs = attention_specs(tokens, rows)
    return pl.pallas_call(
        attend_back_kernel,
        grid=(PAIRS, PAIR_HEADS),
        in_specs=[head, head_t, head, head_t, key_spec, key_spec, line, line] + mark_specs,
        out_specs=[head, key_spec, key_spec],
        out_shape=[
            jax.ShapeDtypeStruct((PAIRS, PAIR_HEADS, PAIR_WIDTH, tokens), F32),
            jax.ShapeDtypeStruct(keys.shape, BF16),
            jax.ShapeDtypeStruct(keys.shape, BF16),
        ],
        scratch_shapes=[
            pltpu.VMEM((rows, tokens), F32),
            pltpu.VMEM((PAIR_WIDTH, rows), BF16),
            pltpu.VMEM((rows, PAIR_WIDTH), F32),
            pltpu.VMEM((rows, PAIR_WIDTH), F32),
        ],
        cost_estimate=pl.CostEstimate(
            flops=10 * QUERY_HEADS * tokens * rows * PAIR_WIDTH,
            bytes_accessed=24 << 20,
            transcendentals=QUERY_HEADS * tokens * rows,
        ),
        name="attend_back",
    )(queries, queries_t, grads, grads_t, keys, values, lse, delta, *marks)


def expert_kernel(
    x_ref, g_ref, w_ref, wi_ref, wo_ref, mix_ref, back_ref, gate_ref, dwi_ref, dwo_ref, dwi, dwo, mid, rows
):
    step = pl.program_id(0)
    count, width = wi_ref.shape[0], wi_ref.shape[1]

    @pl.when(step == 0)
    def _():
        dwi[...] = jnp.zeros_like(dwi)
        dwo[...] = jnp.zeros_like(dwo)

    grad = g_ref[...]
    for e in range(count):
        gate_up = dot(x_ref[...], wi_ref[e])
        gate, up = gate_up[:, :EXPERT_H], gate_up[:, EXPERT_H:]
        sigmoid = 1.0 / (1.0 + jnp.exp(-gate))
        silu = gate * sigmoid
        hidden = (silu * up).astype(BF16).astype(F32)
        weight = w_ref[:, e : e + 1]
        inward = dot_nt(grad, wo_ref[e])
        gate_ref[:, e : e + 1] = jnp.sum(hidden * inward, axis=1, keepdims=True)
        weighted = (weight * hidden).astype(BF16)
        hidden_grad = weight * inward
        mid[:, e * EXPERT_H : (e + 1) * EXPERT_H] = weighted
        at = 2 * e * EXPERT_H
        rows[:, at : at + EXPERT_H] = (
            hidden_grad * up * sigmoid * (1.0 + gate * (1.0 - sigmoid))
        ).astype(BF16)
        rows[:, at + EXPERT_H : at + 2 * EXPERT_H] = (hidden_grad * silu).astype(BF16)
        dwo[e] += dot_tn(weighted, grad)
    tile = 256
    for e in range(count):
        inner = rows[:, 2 * e * EXPERT_H : 2 * (e + 1) * EXPERT_H]

        @pl.loop(0, width // tile)
        def _(t):
            at = pl.multiple_of(t * tile, tile)
            dwi[e, pl.ds(at, tile), :] += dot_tn(x_ref[:, pl.ds(at, tile)], inner)

    @pl.loop(0, width // tile)
    def _(t):
        at = pl.multiple_of(t * tile, tile)
        mixed, back = 0.0, 0.0
        for e in range(count):
            mixed += dot(mid[:, e * EXPERT_H : (e + 1) * EXPERT_H], wo_ref[e, :, pl.ds(at, tile)])
            back += dot_nt(
                rows[:, 2 * e * EXPERT_H : 2 * (e + 1) * EXPERT_H], wi_ref[e, pl.ds(at, tile), :]
            )
        mix_ref[:, pl.ds(at, tile)] = mixed.astype(BF16)
        back_ref[:, pl.ds(at, tile)] = back.astype(BF16)

    @pl.when(step == pl.num_programs(0) - 1)
    def _():
        dwi_ref[...] = dwi[...].astype(BF16)
        dwo_ref[...] = dwo[...].astype(BF16)


def experts_pass(tokens, grads, weights, inner, outer):
    rows, width = tokens.shape
    block = 256
    row_spec = pl.BlockSpec((block, width), lambda i: (i, 0))
    count = inner.shape[0]
    gate_spec = pl.BlockSpec((block, count), lambda i: (i, 0))
    once = pl.Buffered(1)
    inner_spec = pl.BlockSpec(inner.shape, lambda i: (0, 0, 0), pipeline_mode=once)
    outer_spec = pl.BlockSpec(outer.shape, lambda i: (0, 0, 0), pipeline_mode=once)
    return pl.pallas_call(
        expert_kernel,
        grid=(rows // block,),
        in_specs=[row_spec, row_spec, gate_spec, inner_spec, outer_spec],
        out_specs=[row_spec, row_spec, gate_spec, inner_spec, outer_spec],
        out_shape=[
            jax.ShapeDtypeStruct((rows, width), BF16),
            jax.ShapeDtypeStruct((rows, width), BF16),
            jax.ShapeDtypeStruct((rows, count), F32),
            jax.ShapeDtypeStruct(inner.shape, BF16),
            jax.ShapeDtypeStruct(outer.shape, BF16),
        ],
        scratch_shapes=[
            pltpu.VMEM(inner.shape, F32),
            pltpu.VMEM(outer.shape, F32),
            pltpu.VMEM((block, count * EXPERT_H), BF16),
            pltpu.VMEM((block, 2 * count * EXPERT_H), BF16),
        ],
        compiler_params=pltpu.CompilerParams(vmem_limit_bytes=60 << 20),
        cost_estimate=pl.CostEstimate(
            flops=18 * count * rows * width * EXPERT_H,
            bytes_accessed=48 << 20,
            transcendentals=rows * count * EXPERT_H,
        ),
        name="experts",
    )(tokens, grads, weights, inner, outer)


MESH = pl.DeviceIdType.MESH
SLOW = 4
CHUNKS = 2


def ring_position(index, size):
    fast = size // SLOW
    row, column = lax.div(index, fast), lax.rem(index, fast)
    back = SLOW - 1 - row
    odd = lax.rem(back, 2)
    along = (column - 1) * (1 - odd) + (fast - 1 - column) * odd
    away = lax.div(column + fast - 2, fast - 1)
    return (1 - away) * row + away * (SLOW + back * (fast - 1) + along)


def ring_index(position, size):
    fast = size // SLOW
    away = lax.div(lax.div(position, SLOW) + fast - 2, fast - 1)
    rest = away * (position - SLOW)
    back, step = lax.div(rest, fast - 1), lax.rem(rest, fast - 1)
    odd = lax.rem(back, 2)
    column = (1 + step) * (1 - odd) + (fast - 1 - step) * odd
    return (1 - away) * position * fast + away * ((SLOW - 1 - back) * fast + column)


class Ring:
    def __init__(self, size):
        self.size, self.steps = size, size // 2
        self.me = lax.axis_index("ctx")
        self.place = ring_position(self.me, size)

    def at(self, shift):
        return ring_index(lax.rem(self.place + shift + self.size, self.size), self.size)

    def toward(self, direction, distance):
        return self.at(distance if direction == 0 else -distance)

    def device(self, direction):
        return (self.toward(direction, 1), lax.axis_index("wsh"))

    def meet(self):
        barrier = pltpu.get_barrier_semaphore()
        for direction in range(2):
            pl.semaphore_signal(
                barrier, inc=1, device_id=self.device(direction), device_id_type=MESH
            )
        pl.semaphore_wait(barrier, 2)

    def chunks(self, direction, last):
        if not last:
            return range(CHUNKS)
        half = CHUNKS // 2
        return range(half) if direction == 0 else range(half, CHUNKS)


def rows_at(block, rows, chunk):
    part = rows // CHUNKS
    return pl.ds(pl.multiple_of(block * rows + chunk * part, part), part)


def ring_gather_kernel(size, count, *refs):
    locals_, outs = refs[:count], refs[count : 2 * count]
    send, recv, own = refs[2 * count :]
    ring = Ring(size)
    ring.meet()

    def copy(k, direction, step, chunk, block):
        rows = locals_[k].shape[0]
        source = (
            locals_[k].at[rows_at(0, rows, chunk)]
            if step == 0
            else outs[k].at[rows_at(block, rows, chunk)]
        )
        return pltpu.make_async_remote_copy(
            src_ref=source,
            dst_ref=outs[k].at[rows_at(block, rows, chunk)],
            send_sem=send.at[k, direction, step, chunk],
            recv_sem=recv.at[k, direction, step, chunk],
            device_id=ring.device(direction),
            device_id_type=MESH,
        )

    started = []
    kept = []
    for step in range(ring.steps):
        for chunk in range(CHUNKS):
            for direction in range(2):
                if step > 0:
                    for k in range(count):
                        block = ring.toward(1 - direction, step)
                        copy(k, direction, step - 1, chunk, block).wait_recv()
                if chunk in ring.chunks(direction, step == ring.steps - 1):
                    for k in range(count):
                        moved = copy(k, direction, step, chunk, ring.toward(1 - direction, step))
                        moved.start()
                        started.append(moved)
        if step == 0:
            for k in range(count):
                rows = locals_[k].shape[0]
                place = pl.ds(pl.multiple_of(ring.me * rows, rows), rows)
                kept.append(pltpu.make_async_copy(locals_[k], outs[k].at[place], own.at[k]))
                kept[-1].start()
    last = ring.steps - 1
    for direction in range(2):
        for chunk in ring.chunks(direction, True):
            for k in range(count):
                copy(k, direction, last, chunk, ring.toward(1 - direction, last + 1)).wait_recv()
    for moved in started:
        moved.wait_send()
    for moved in kept:
        moved.wait()


def ring_gather(arrays, size, identity, name):
    count = len(arrays)
    sems = pltpu.SemaphoreType.DMA((count, 2, size // 2, CHUNKS))
    return pl.pallas_call(
        functools.partial(ring_gather_kernel, size, count),
        in_specs=[pl.BlockSpec(memory_space=pltpu.VMEM)] * count,
        out_specs=[pl.BlockSpec(memory_space=pl.ANY)] * count,
        out_shape=[
            jax.ShapeDtypeStruct((size * a.shape[0],) + a.shape[1:], a.dtype) for a in arrays
        ],
        scratch_shapes=[sems, sems, pltpu.SemaphoreType.DMA((count,))],
        compiler_params=pltpu.CompilerParams(collective_id=identity, has_side_effects=True),
        cost_estimate=pl.CostEstimate(flops=0, bytes_accessed=100 << 20, transcendentals=0),
        name=name,
    )(*arrays)


def ring_scatter_kernel(size, count, *refs):
    parts, outs = refs[:count], refs[count : 2 * count]
    stages, lands = refs[2 * count : 3 * count], refs[3 * count : 4 * count]
    send, recv = refs[4 * count :]
    ring = Ring(size)
    ring.meet()

    def copy(k, direction, step, chunk):
        rows = outs[k].shape[0]
        if step == 0:
            source = parts[k].at[rows_at(ring.toward(direction, ring.steps), rows, chunk)]
        else:
            source = stages[k].at[direction, step - 1, rows_at(0, rows, chunk)]
        return pltpu.make_async_remote_copy(
            src_ref=source,
            dst_ref=lands[k].at[direction, step, rows_at(0, rows, chunk)],
            send_sem=send.at[k, direction, step, chunk],
            recv_sem=recv.at[k, direction, step, chunk],
            device_id=ring.device(direction),
            device_id_type=MESH,
        )

    started = []
    for step in range(ring.steps):
        for chunk in range(CHUNKS):
            for direction in range(2):
                for k in range(count):
                    rows = outs[k].shape[0]
                    if step == 0:
                        if chunk not in ring.chunks(direction, True):
                            continue
                    else:
                        here = rows_at(0, rows, chunk)
                        dest = ring.toward(direction, ring.steps - step)
                        total = parts[k][rows_at(dest, rows, chunk)]
                        if step > 1 or chunk in ring.chunks(direction, True):
                            copy(k, direction, step - 1, chunk).wait_recv()
                            landed = lands[k][direction, step - 1, here]
                            total = (total.astype(F32) + landed.astype(F32)).astype(total.dtype)
                        stages[k][direction, step - 1, here] = total
                    moved = copy(k, direction, step, chunk)
                    moved.start()
                    started.append(moved)
    last = ring.steps - 1
    for chunk in range(CHUNKS):
        for k in range(count):
            rows = outs[k].shape[0]
            here = rows_at(0, rows, chunk)
            total = parts[k][rows_at(ring.me, rows, chunk)].astype(F32)
            for direction in range(2):
                copy(k, direction, last, chunk).wait_recv()
                total += lands[k][direction, last, here].astype(F32)
            outs[k][here] = total
    for moved in started:
        moved.wait_send()


def ring_scatter(arrays, size, identity, name):
    count, steps = len(arrays), size // 2
    sems = pltpu.SemaphoreType.DMA((count, 2, steps, CHUNKS))
    blocks = [(a.shape[0] // size,) + a.shape[1:] for a in arrays]
    vmem = pl.BlockSpec(memory_space=pltpu.VMEM)
    return pl.pallas_call(
        functools.partial(ring_scatter_kernel, size, count),
        in_specs=[vmem] * count,
        out_specs=[vmem] * count,
        out_shape=[jax.ShapeDtypeStruct(b, F32) for b in blocks],
        scratch_shapes=[
            pltpu.VMEM((2, steps - 1) + b, a.dtype) for a, b in zip(arrays, blocks)
        ]
        + [pltpu.VMEM((2, steps) + b, a.dtype) for a, b in zip(arrays, blocks)]
        + [sems, sems],
        compiler_params=pltpu.CompilerParams(
            collective_id=identity, has_side_effects=True, vmem_limit_bytes=48 << 20
        ),
        cost_estimate=pl.CostEstimate(flops=0, bytes_accessed=100 << 20, transcendentals=0),
        name=name,
    )(*arrays)


EXTRA = 16


def reduce_kernel(
    size, shards, lhs, rhs, small, out, part, cores, lines, total, stage, land, held,
    core_send, core_recv, line_send, line_recv, ring_send, ring_recv, all_send, all_recv,
):
    ring = Ring(size)
    steps, height = ring.steps, shards // 2
    spot = lax.axis_index("wsh")
    core, row = lax.rem(spot, 2), lax.div(spot, 2)
    ctx = ring.me
    slot_rows, width = total.shape[1], total.shape[2]
    shard_rows = slot_rows - EXTRA
    split = width // CHUNKS
    mate = (ctx, row * 2 + 1 - core)
    above = (ctx, lax.rem(row + 1, height) * 2 + core)
    below = (ctx, lax.rem(row + height - 1, height) * 2 + core)

    barrier = pltpu.get_barrier_semaphore()
    for device in (mate, above, below, ring.device(0), ring.device(1)):
        pl.semaphore_signal(barrier, inc=1, device_id=device, device_id_type=MESH)
    pl.semaphore_wait(barrier, 5)

    order = [steps]
    for distance in range(steps - 1, 0, -1):
        order += [distance, -distance]
    order.append(0)
    slot_of = {shift: i for i, shift in enumerate(order)}
    slot_of[-steps] = 0
    blocks = [ring.at(shift) for shift in order]
    started = []

    def begin(copy):
        copy.start()
        started.append(copy)

    def remote(source, target, send, recv, device):
        return pltpu.make_async_remote_copy(
            src_ref=source,
            dst_ref=target,
            send_sem=send,
            recv_sem=recv,
            device_id=device,
            device_id_type=MESH,
        )

    def to_mate(i, y):
        return remote(
            part.at[i, y * 2 + 1 - core], cores.at[i, y], core_send.at[i, y], core_recv.at[i, y], mate
        )

    def to_line(i, t):
        shard = lax.rem(row + 2 * height - 1 - t, height) * 2 + core
        return remote(
            part.at[i, shard], lines.at[i, t], line_send.at[i, t], line_recv.at[i, t], above
        )

    def form(i):
        at = pl.multiple_of(blocks[i] * width, width)
        side = lax.div(blocks[i] * width, lhs.shape[1] + 2 * KEY_HEADS * HEAD_SIZE)

        @pl.loop(0, shards)
        def _(w):
            rows = pl.ds(pl.multiple_of(w * shard_rows, shard_rows), shard_rows)
            product = dot(lhs[side, rows, :], rhs[:, pl.ds(at, width)])
            part[i, w, :shard_rows, :] = product.astype(BF16)
            part[i, w, shard_rows:, :] = small[w, :, pl.ds(at, width)]

        for y in range(height):
            begin(to_mate(i, y))

    def add_cores(i):
        for y in range(height):
            to_mate(i, y).wait_recv()
            both = part[i, y * 2 + core].astype(F32) + cores[i, y].astype(F32)
            part[i, y * 2 + core] = both.astype(BF16)
        begin(to_line(i, 0))

    for i in range(size):
        form(i)
        if i > 0:
            add_cores(i - 1)
    add_cores(size - 1)
    for t in range(1, height - 1):
        for i in range(size):
            to_line(i, t - 1).wait_recv()
            shard = lax.rem(row + 2 * height - 1 - t, height) * 2 + core
            both = part[i, shard].astype(F32) + lines[i, t - 1].astype(F32)
            part[i, shard] = both.astype(BF16)
            begin(to_line(i, t))

    def finish_line(i):
        to_line(i, height - 2).wait_recv()
        total[i] = part[i, spot].astype(F32) + lines[i, height - 2].astype(F32)

    def columns(chunk):
        return pl.ds(chunk * split, split)

    def around(direction, step, chunk):
        return remote(
            stage.at[direction, step, :, columns(chunk)],
            land.at[direction, step, :, columns(chunk)],
            ring_send.at[direction, step, chunk],
            ring_recv.at[direction, step, chunk],
            ring.device(direction),
        )

    for step in range(steps):
        reach = steps - step
        for i in sorted({slot_of[reach], slot_of[-reach]}):
            finish_line(i)
        for chunk in range(CHUNKS):
            for direction in range(2):
                if step == 0 and chunk not in ring.chunks(direction, True):
                    continue
                at = columns(chunk)
                value = total[slot_of[reach if direction == 0 else -reach], :, at]
                if step > 1 or (step == 1 and chunk in ring.chunks(direction, True)):
                    around(direction, step - 1, chunk).wait_recv()
                    value += land[direction, step - 1, :, at].astype(F32)
                stage[direction, step, :, at] = value.astype(BF16)
                begin(around(direction, step, chunk))

    def onward(direction, step, chunk, block):
        return remote(
            held.at[block, :, columns(chunk)],
            held.at[block, :, columns(chunk)],
            all_send.at[direction, step, chunk],
            all_recv.at[direction, step, chunk],
            ring.device(direction),
        )

    def put(block, chunk):
        at = pl.ds(pl.multiple_of(block * width + chunk * split, split), split)
        out[:, at] = held[block, :, columns(chunk)].astype(F32)

    own = slot_of[0]
    finish_line(own)
    for chunk in range(CHUNKS):
        at = columns(chunk)
        value = total[own, :, at]
        for direction in range(2):
            around(direction, steps - 1, chunk).wait_recv()
            value += land[direction, steps - 1, :, at].astype(F32)
        held[ctx, :, at] = value.astype(BF16)
        for direction in range(2):
            begin(onward(direction, 0, chunk, ctx))
    for chunk in range(CHUNKS):
        put(ctx, chunk)
    for step in range(1, steps + 1):
        for chunk in range(CHUNKS):
            for direction in range(2):
                if step == steps and chunk not in ring.chunks(direction, True):
                    continue
                block = ring.toward(1 - direction, step)
                onward(direction, step - 1, chunk, block).wait_recv()
                if step < steps and chunk in ring.chunks(direction, step == steps - 1):
                    begin(onward(direction, step, chunk, block))
                put(block, chunk)
    for copy in started:
        copy.wait_send()


def reduce_grads(lhs, rhs, small, size, shards, identity):
    steps, height = size // 2, shards // 2
    columns = rhs.shape[1]
    width, rows = columns // size, lhs.shape[1] // shards + EXTRA
    vmem = pl.BlockSpec(memory_space=pltpu.VMEM)
    dma = pltpu.SemaphoreType.DMA
    return pl.pallas_call(
        functools.partial(reduce_kernel, size, shards),
        in_specs=[vmem] * 3,
        out_specs=vmem,
        out_shape=jax.ShapeDtypeStruct((rows, columns), F32),
        scratch_shapes=[
            pltpu.VMEM((size, shards, rows, width), BF16),
            pltpu.VMEM((size, height, rows, width), BF16),
            pltpu.VMEM((size, height - 1, rows, width), BF16),
            pltpu.VMEM((size, rows, width), F32),
            pltpu.VMEM((2, steps, rows, width), BF16),
            pltpu.VMEM((2, steps, rows, width), BF16),
            pltpu.VMEM((size, rows, width), BF16),
            dma((size, height)),
            dma((size, height)),
            dma((size, height - 1)),
            dma((size, height - 1)),
        ]
        + [dma((2, steps, CHUNKS))] * 4,
        compiler_params=pltpu.CompilerParams(
            collective_id=identity, has_side_effects=True, vmem_limit_bytes=62 << 20
        ),
        cost_estimate=pl.CostEstimate(
            flops=2 * lhs.shape[1] * lhs.shape[2] * columns,
            bytes_accessed=300 << 20,
            transcendentals=0,
        ),
        name="reduce_grads",
    )(lhs, rhs, small)


def on_device(
    layer_input,
    attention_gain,
    query_weight,
    key_matrix,
    value_matrix,
    output_weight,
    expert_gain,
    router_weight,
    expert_inner,
    expert_outer,
    document_lengths,
    token_places,
    expert_routes,
    cotangent,
):
    group_devices = lax.axis_size("ctx")
    ctx_index = lax.axis_index("ctx")
    token_rows = layer_input.shape[1]
    experts = router_weight.shape[1]
    own_experts = expert_inner.shape[0]
    key_value_width = KEY_HEADS * HEAD_SIZE

    def gather(shard, axis=0):
        return lax.all_gather(shard, "wsh", axis=axis, tiled=True)

    small = gather(
        jnp.concatenate([attention_gain[:, None], expert_gain[:, None], router_weight], axis=1)
    )
    gain_one, gain_two = small[:, 0].astype(F32), small[:, 1].astype(F32)
    whole_router = small[:, 2:]
    whole_key = gather(key_matrix)
    whole_value = gather(value_matrix)
    whole_query = gather(query_weight)
    whole_output = gather(output_weight)
    whole_inner = gather(expert_inner, 1)
    whole_outer = gather(expert_outer, 1)
    all_grads = lax.all_gather(cotangent[0], "ctx", axis=0, tiled=True)

    places_all = token_places[0]
    key_documents, key_offsets = locate(document_lengths[0], places_all)
    first_row = ctx_index * token_rows
    query_places = lax.dynamic_slice_in_dim(places_all, first_row, token_rows)
    query_documents = lax.dynamic_slice_in_dim(key_documents, first_row, token_rows)
    query_offsets = lax.dynamic_slice_in_dim(key_offsets, first_row, token_rows)
    marks = (
        key_documents[:, None],
        places_all[:, None],
        query_documents[None, :],
        query_places[None, :],
    )
    cosine_rows, sine_table = angles_for(query_offsets)

    inputs_f = layer_input[0].astype(F32)
    inverse_one = rms_inverse(inputs_f)
    normed_one = (inputs_f * inverse_one * gain_one).astype(BF16)
    key_pre = dot(normed_one, whole_key)
    keys = (
        apply_rotation(key_pre.reshape(token_rows, KEY_HEADS, HEAD_SIZE), cosine_rows, sine_table)
        .astype(BF16)
        .reshape(token_rows, key_value_width)
    )
    values = dot(normed_one, whole_value).astype(BF16)
    all_keys, all_values = ring_gather([keys, values], group_devices, 1, "gather_keys")
    query_pre = dot(normed_one, whole_query)
    queries = (
        apply_rotation(
            query_pre.reshape(token_rows, QUERY_HEADS, HEAD_SIZE), cosine_rows, sine_table
        ).astype(BF16)
        * SCALE
    ).reshape(token_rows, QUERY_HEADS * HEAD_SIZE)
    spread_queries = spread_heads(queries)
    spread_attended, lse = attend(spread_queries, all_keys, all_values, marks)
    attended_f = gather_heads(spread_attended)
    attended = attended_f.astype(BF16)
    residual = inputs_f + dot(attended, whole_output)
    inverse_two = rms_inverse(residual)
    normed_two = (residual * inverse_two * gain_two).astype(BF16)
    logits = dot(normed_two, whole_router)
    expert_ids = jnp.arange(experts, dtype=jnp.int32)
    routed = jnp.any(expert_routes[0][:, :, None] == expert_ids[None, None, :], axis=1)
    gates = jax.nn.softmax(jnp.where(routed, logits, -jnp.inf), axis=-1)

    all_tokens, all_gates = ring_gather([normed_two, gates.T], group_devices, 2, "gather_tokens")
    own_gates = (
        lax.dynamic_slice_in_dim(
            all_gates.reshape(group_devices, experts, token_rows),
            ctx_index * own_experts,
            own_experts,
            axis=1,
        )
        .transpose(0, 2, 1)
        .reshape(group_devices * token_rows, own_experts)
    )
    mixed, back_rows, own_gate_grad, inner_grad, outer_grad = experts_pass(
        all_tokens, all_grads, own_gates, whole_inner, whole_outer
    )
    placed = lax.dynamic_update_slice_in_dim(
        jnp.zeros((group_devices, experts, token_rows), F32),
        own_gate_grad.reshape(group_devices, token_rows, own_experts).transpose(0, 2, 1),
        ctx_index * own_experts,
        axis=1,
    ).reshape(group_devices * experts, token_rows)
    back_sum, gate_grad = ring_scatter([back_rows, placed], group_devices, 3, "scatter_rows")
    gate_grad = gate_grad.T
    mixture = lax.psum_scatter(mixed, "ctx", scatter_dimension=0, tiled=True)
    layer_output = (residual + mixture.astype(F32)).astype(BF16)

    out_grad = cotangent[0].astype(F32)
    logit_grad = (
        gates * (gate_grad - jnp.sum(gates * gate_grad, axis=-1, keepdims=True))
    ).astype(BF16)
    router_grad = dot_tn(normed_two, logit_grad)
    normed_two_grad = dot_nt(logit_grad, whole_router) + back_sum
    gain_two_grad, residual_back = norm_backward(residual, inverse_two, gain_two, normed_two_grad)
    residual_grad = out_grad + residual_back
    branch_grad = residual_grad.astype(BF16)
    attended_grad = dot_nt(branch_grad, whole_output).astype(BF16)
    delta = jnp.sum(
        (attended_grad.astype(F32) * attended_f).reshape(token_rows, QUERY_HEADS, HEAD_SIZE), axis=-1
    ).T.reshape(PAIRS, PAIR_HEADS, 1, token_rows)
    spread_grads = spread_heads(attended_grad)
    spread_query_grad, key_part, value_part = attend_back(
        spread_queries,
        spread_queries.transpose(0, 1, 3, 2),
        spread_grads,
        spread_grads.transpose(0, 1, 3, 2),
        all_keys,
        all_values,
        lse,
        delta,
        marks,
    )
    key_grad, value_grad = ring_scatter([key_part, value_part], group_devices, 4, "scatter_keys")
    value_grad = value_grad.astype(BF16)
    query_pre_grad = (
        reverse_rotation(
            (gather_heads(spread_query_grad) * SCALE).reshape(token_rows, QUERY_HEADS, HEAD_SIZE),
            cosine_rows,
            sine_table,
        )
        .reshape(token_rows, QUERY_HEADS * HEAD_SIZE)
        .astype(BF16)
    )
    key_pre_grad = (
        reverse_rotation(
            key_grad.reshape(token_rows, KEY_HEADS, HEAD_SIZE), cosine_rows, sine_table
        )
        .reshape(token_rows, key_value_width)
        .astype(BF16)
    )
    normed_one_grad = (
        dot_nt(query_pre_grad, whole_query)
        + dot_nt(key_pre_grad, whole_key)
        + dot_nt(value_grad, whole_value)
    )
    gain_one_grad, input_back = norm_backward(inputs_f, inverse_one, gain_one, normed_one_grad)
    input_grad = residual_grad + input_back

    def scatter(grad, dim=0):
        return lax.psum_scatter(grad.astype(BF16), "wsh", scatter_dimension=dim, tiled=True)

    inner_out = scatter(inner_grad, 1).astype(F32)
    outer_out = scatter(outer_grad, 1).astype(F32)
    shards = lax.axis_size("wsh")
    shard_rows = query_weight.shape[0]
    columns = 2 * query_weight.shape[1] + 2 * key_value_width
    marks_small = jnp.concatenate(
        [gain_one_grad[None], gain_two_grad[None], router_grad.T], axis=0
    ).astype(BF16)
    small_count = marks_small.shape[0]
    small_rows = marks_small.reshape(small_count, shards, shard_rows).transpose(1, 0, 2)
    small_rows = small_rows.reshape(shards, small_count * shard_rows)
    across = -(-small_count * shard_rows // EXTRA // 128) * 128
    small_rows = jnp.pad(small_rows, ((0, 0), (0, EXTRA * across - small_rows.shape[1])))
    small_rows = jnp.pad(
        small_rows.reshape(shards, EXTRA, across), ((0, 0), (0, 0), (0, columns - across))
    )
    summed = reduce_grads(
        jnp.stack([normed_one.T, attended.T]),
        jnp.concatenate([query_pre_grad, key_pre_grad, value_grad, branch_grad], axis=1),
        small_rows,
        group_devices,
        shards,
        5,
    )
    small_out = summed[shard_rows:, :across].reshape(-1)[: small_count * shard_rows]
    small_out = small_out.reshape(small_count, shard_rows)
    ends = [0]
    for shard in (query_weight, key_matrix, value_matrix, output_weight):
        ends.append(ends[-1] + shard.shape[1])
    query_out, key_out, value_out, output_out = (
        summed[:shard_rows, start:end] for start, end in zip(ends, ends[1:])
    )
    return (
        layer_output[None],
        input_grad[None],
        small_out[0],
        query_out,
        key_out,
        value_out,
        output_out,
        small_out[1],
        small_out[2:].T,
        inner_out,
        outer_out,
    )


def solution(mesh):
    tokens = P("wsh", "ctx", None)
    shard, expert = P("wsh", None), P("ctx", "wsh", None)
    return jax.shard_map(
        on_device,
        mesh=mesh,
        in_specs=(
            tokens,
            P("wsh"),
            shard,
            shard,
            shard,
            shard,
            P("wsh"),
            shard,
            expert,
            expert,
            shard,
            shard,
            tokens,
            tokens,
        ),
        out_specs=(
            tokens,
            tokens,
            P("wsh"),
            shard,
            shard,
            shard,
            shard,
            P("wsh"),
            shard,
            expert,
            expert,
        ),
        check_vma=False,
    )
```

```python
import functools

import jax
import jax.numpy as jnp
from jax import lax
from jax.experimental import pallas as pl
from jax.experimental.pallas import tpu as pltpu
from jax.sharding import PartitionSpec as P

QUERY_HEADS = 24
KEY_HEADS = 8
HEAD_SIZE = 64
EXPERT_H = 512
TOPK = 8
SEQS = 4
GROUP = QUERY_HEADS // KEY_HEADS
PAIRS = KEY_HEADS // 2
PAIR_HEADS = 2 * GROUP
PAIR_WIDTH = 2 * HEAD_SIZE

EPS = 1e-05
THETA = 10000.0
MASK_FILL = -1e30
SCALE = HEAD_SIZE**-0.5
BF16 = jnp.bfloat16
F32 = jnp.float32


def dot(a, b):
    return jnp.dot(a, b, preferred_element_type=F32)


def dot_nt(a, b):
    return lax.dot_general(a, b, (((1,), (1,)), ((), ())), preferred_element_type=F32)


def dot_tn(a, b):
    return lax.dot_general(a, b, (((0,), (0,)), ((), ())), preferred_element_type=F32)


def rms_inverse(matrix):
    return lax.rsqrt(jnp.mean(matrix * matrix, axis=-1, keepdims=True) + EPS)


def locate(lengths_row, places_row):
    segment_ends = jnp.cumsum(lengths_row)
    beyond = (places_row[:, None] >= segment_ends[None, :]).astype(jnp.int32)
    documents = jnp.sum(beyond, axis=1)
    offsets = places_row - jnp.sum(beyond * lengths_row[None, :], axis=1)
    return (documents, offsets)


def angles_for(offsets):
    halfway = HEAD_SIZE // 2
    frequency = THETA ** (-2.0 * jnp.arange(halfway, dtype=F32) / HEAD_SIZE)
    angles = offsets.astype(F32)[:, None] * frequency[None, :]
    return (jnp.cos(angles)[:, None, :], jnp.sin(angles)[:, None, :])


def apply_rotation(matrix, cosine_rows, sine_table):
    halfway = matrix.shape[-1] // 2
    former = matrix[..., :halfway]
    latter = matrix[..., halfway:]
    return jnp.concatenate(
        [former * cosine_rows - latter * sine_table, latter * cosine_rows + former * sine_table],
        axis=-1,
    )


def reverse_rotation(matrix, cosine_rows, sine_table):
    return apply_rotation(matrix, cosine_rows, -sine_table)


def norm_backward(matrix, inverse, gains, gradients):
    scaled = gradients * gains
    gain_grad = jnp.sum(gradients * matrix * inverse, axis=0)
    input_back = inverse * scaled - matrix * inverse * inverse * inverse * jnp.mean(
        scaled * matrix, axis=-1, keepdims=True
    )
    return (gain_grad, input_back)


def spread_heads(rows):
    tokens = rows.shape[0]
    heads = rows.reshape(tokens, PAIRS, 2, GROUP, HEAD_SIZE).transpose(1, 2, 3, 4, 0)
    zero = jnp.zeros_like(heads[:, 0])
    low = jnp.concatenate([heads[:, 0], zero], axis=2)
    high = jnp.concatenate([zero, heads[:, 1]], axis=2)
    return jnp.stack([low, high], axis=1).reshape(PAIRS, PAIR_HEADS, PAIR_WIDTH, tokens)


def gather_heads(spread):
    tokens = spread.shape[-1]
    split = spread.reshape(PAIRS, 2, GROUP, 2, HEAD_SIZE, tokens)
    heads = jnp.stack([split[:, 0, :, 0], split[:, 1, :, 1]], axis=1)
    return heads.transpose(4, 0, 1, 2, 3).reshape(tokens, QUERY_HEADS * HEAD_SIZE)


def fill_bias(bias_ref, kdoc_ref, kplace_ref, qdoc_ref, qplace_ref):
    kdoc, kplace = kdoc_ref[...], kplace_ref[...]
    qdoc, qplace = qdoc_ref[...], qplace_ref[...]
    seen = (kdoc == qdoc) & (qdoc < SEQS) & (kplace <= qplace) | (kplace == qplace)
    bias_ref[...] = jnp.where(seen, 0.0, MASK_FILL)


def attend_kernel(
    q_ref, k_ref, v_ref, kdoc_ref, kplace_ref, qdoc_ref, qplace_ref, o_ref, lse_ref, bias, vt
):
    pair, head = pl.program_id(0), pl.program_id(1)

    @pl.when((pair == 0) & (head == 0))
    def _():
        fill_bias(bias, kdoc_ref, kplace_ref, qdoc_ref, qplace_ref)

    @pl.when(head == 0)
    def _():
        vt[...] = v_ref[...].T

    scores = dot(k_ref[...], q_ref[0, 0]) + bias[...]
    top = jnp.max(scores, axis=0, keepdims=True)
    weights = jnp.exp(scores - top)
    total = jnp.sum(weights, axis=0, keepdims=True)
    o_ref[0, 0] = dot(vt[...], weights.astype(BF16)) / total
    lse_ref[0, 0] = top + jnp.log(total)


def attend_back_kernel(
    q_ref,
    qt_ref,
    g_ref,
    gt_ref,
    k_ref,
    v_ref,
    lse_ref,
    delta_ref,
    kdoc_ref,
    kplace_ref,
    qdoc_ref,
    qplace_ref,
    dq_ref,
    dk_ref,
    dv_ref,
    bias,
    kt,
    dk_sum,
    dv_sum,
):
    pair, head = pl.program_id(0), pl.program_id(1)

    @pl.when((pair == 0) & (head == 0))
    def _():
        fill_bias(bias, kdoc_ref, kplace_ref, qdoc_ref, qplace_ref)

    @pl.when(head == 0)
    def _():
        kt[...] = k_ref[...].T
        dk_sum[...] = jnp.zeros_like(dk_sum)
        dv_sum[...] = jnp.zeros_like(dv_sum)

    scores = dot(k_ref[...], q_ref[0, 0]) + bias[...]
    probs = jnp.exp(scores - lse_ref[0, 0])
    prob_grad = dot(v_ref[...], g_ref[0, 0])
    score_grad = (probs * (prob_grad - delta_ref[0, 0])).astype(BF16)
    dv_sum[...] += dot(probs.astype(BF16), gt_ref[0, 0])
    dk_sum[...] += dot(score_grad, qt_ref[0, 0])
    dq_ref[0, 0] = dot(kt[...], score_grad)

    @pl.when(head == PAIR_HEADS - 1)
    def _():
        dk_ref[...] = dk_sum[...].astype(BF16)
        dv_ref[...] = dv_sum[...].astype(BF16)


def whole(shape):
    return pl.BlockSpec(shape, lambda *_: (0,) * len(shape))


def attention_specs(tokens, rows):
    head = pl.BlockSpec((1, 1, PAIR_WIDTH, tokens), lambda p, h: (p, h, 0, 0))
    head_t = pl.BlockSpec((1, 1, tokens, PAIR_WIDTH), lambda p, h: (p, h, 0, 0))
    line = pl.BlockSpec((1, 1, 1, tokens), lambda p, h: (p, h, 0, 0))
    keys = pl.BlockSpec((rows, PAIR_WIDTH), lambda p, h: (0, p))
    marks = [whole((rows, 1)), whole((rows, 1)), whole((1, tokens)), whole((1, tokens))]
    return head, head_t, line, keys, marks


def attend(queries, keys, values, marks):
    tokens, rows = queries.shape[-1], keys.shape[0]
    head, _, line, key_spec, mark_specs = attention_specs(tokens, rows)
    return pl.pallas_call(
        attend_kernel,
        grid=(PAIRS, PAIR_HEADS),
        in_specs=[head, key_spec, key_spec] + mark_specs,
        out_specs=[head, line],
        out_shape=[
            jax.ShapeDtypeStruct((PAIRS, PAIR_HEADS, PAIR_WIDTH, tokens), F32),
            jax.ShapeDtypeStruct((PAIRS, PAIR_HEADS, 1, tokens), F32),
        ],
        scratch_shapes=[pltpu.VMEM((rows, tokens), F32), pltpu.VMEM((PAIR_WIDTH, rows), BF16)],
        cost_estimate=pl.CostEstimate(
            flops=4 * QUERY_HEADS * tokens * rows * PAIR_WIDTH,
            bytes_accessed=16 << 20,
            transcendentals=QUERY_HEADS * tokens * rows,
        ),
        name="attend",
    )(queries, keys, values, *marks)


def attend_back(queries, queries_t, grads, grads_t, keys, values, lse, delta, marks):
    tokens, rows = queries.shape[-1], keys.shape[0]
    head, head_t, line, key_spec, mark_specs = attention_specs(tokens, rows)
    return pl.pallas_call(
        attend_back_kernel,
        grid=(PAIRS, PAIR_HEADS),
        in_specs=[head, head_t, head, head_t, key_spec, key_spec, line, line] + mark_specs,
        out_specs=[head, key_spec, key_spec],
        out_shape=[
            jax.ShapeDtypeStruct((PAIRS, PAIR_HEADS, PAIR_WIDTH, tokens), F32),
            jax.ShapeDtypeStruct(keys.shape, BF16),
            jax.ShapeDtypeStruct(keys.shape, BF16),
        ],
        scratch_shapes=[
            pltpu.VMEM((rows, tokens), F32),
            pltpu.VMEM((PAIR_WIDTH, rows), BF16),
            pltpu.VMEM((rows, PAIR_WIDTH), F32),
            pltpu.VMEM((rows, PAIR_WIDTH), F32),
        ],
        cost_estimate=pl.CostEstimate(
            flops=10 * QUERY_HEADS * tokens * rows * PAIR_WIDTH,
            bytes_accessed=24 << 20,
            transcendentals=QUERY_HEADS * tokens * rows,
        ),
        name="attend_back",
    )(queries, queries_t, grads, grads_t, keys, values, lse, delta, *marks)


def expert_kernel(
    x_ref, g_ref, w_ref, wi_ref, wo_ref, mix_ref, back_ref, gate_ref, dwi_ref, dwo_ref, dwi, dwo, mid, rows
):
    step = pl.program_id(0)
    count, width = wi_ref.shape[0], wi_ref.shape[1]

    @pl.when(step == 0)
    def _():
        dwi[...] = jnp.zeros_like(dwi)
        dwo[...] = jnp.zeros_like(dwo)

    grad = g_ref[...]
    for e in range(count):
        gate_up = dot(x_ref[...], wi_ref[e])
        gate, up = gate_up[:, :EXPERT_H], gate_up[:, EXPERT_H:]
        sigmoid = 1.0 / (1.0 + jnp.exp(-gate))
        silu = gate * sigmoid
        hidden = (silu * up).astype(BF16).astype(F32)
        weight = w_ref[:, e : e + 1]
        inward = dot_nt(grad, wo_ref[e])
        gate_ref[:, e : e + 1] = jnp.sum(hidden * inward, axis=1, keepdims=True)
        weighted = (weight * hidden).astype(BF16)
        hidden_grad = weight * inward
        mid[:, e * EXPERT_H : (e + 1) * EXPERT_H] = weighted
        at = 2 * e * EXPERT_H
        rows[:, at : at + EXPERT_H] = (
            hidden_grad * up * sigmoid * (1.0 + gate * (1.0 - sigmoid))
        ).astype(BF16)
        rows[:, at + EXPERT_H : at + 2 * EXPERT_H] = (hidden_grad * silu).astype(BF16)
        dwo[e] += dot_tn(weighted, grad)
    tile = 256
    for e in range(count):
        inner = rows[:, 2 * e * EXPERT_H : 2 * (e + 1) * EXPERT_H]

        @pl.loop(0, width // tile)
        def _(t):
            at = pl.multiple_of(t * tile, tile)
            dwi[e, pl.ds(at, tile), :] += dot_tn(x_ref[:, pl.ds(at, tile)], inner)

    @pl.loop(0, width // tile)
    def _(t):
        at = pl.multiple_of(t * tile, tile)
        mixed, back = 0.0, 0.0
        for e in range(count):
            mixed += dot(mid[:, e * EXPERT_H : (e + 1) * EXPERT_H], wo_ref[e, :, pl.ds(at, tile)])
            back += dot_nt(
                rows[:, 2 * e * EXPERT_H : 2 * (e + 1) * EXPERT_H], wi_ref[e, pl.ds(at, tile), :]
            )
        mix_ref[:, pl.ds(at, tile)] = mixed.astype(BF16)
        back_ref[:, pl.ds(at, tile)] = back.astype(BF16)

    @pl.when(step == pl.num_programs(0) - 1)
    def _():
        dwi_ref[...] = dwi[...].astype(BF16)
        dwo_ref[...] = dwo[...].astype(BF16)


def experts_pass(tokens, grads, weights, inner, outer):
    rows, width = tokens.shape
    block = 256
    row_spec = pl.BlockSpec((block, width), lambda i: (i, 0))
    count = inner.shape[0]
    gate_spec = pl.BlockSpec((block, count), lambda i: (i, 0))
    once = pl.Buffered(1)
    inner_spec = pl.BlockSpec(inner.shape, lambda i: (0, 0, 0), pipeline_mode=once)
    outer_spec = pl.BlockSpec(outer.shape, lambda i: (0, 0, 0), pipeline_mode=once)
    return pl.pallas_call(
        expert_kernel,
        grid=(rows // block,),
        in_specs=[row_spec, row_spec, gate_spec, inner_spec, outer_spec],
        out_specs=[row_spec, row_spec, gate_spec, inner_spec, outer_spec],
        out_shape=[
            jax.ShapeDtypeStruct((rows, width), BF16),
            jax.ShapeDtypeStruct((rows, width), BF16),
            jax.ShapeDtypeStruct((rows, count), F32),
            jax.ShapeDtypeStruct(inner.shape, BF16),
            jax.ShapeDtypeStruct(outer.shape, BF16),
        ],
        scratch_shapes=[
            pltpu.VMEM(inner.shape, F32),
            pltpu.VMEM(outer.shape, F32),
            pltpu.VMEM((block, count * EXPERT_H), BF16),
            pltpu.VMEM((block, 2 * count * EXPERT_H), BF16),
        ],
        compiler_params=pltpu.CompilerParams(vmem_limit_bytes=60 << 20),
        cost_estimate=pl.CostEstimate(
            flops=18 * count * rows * width * EXPERT_H,
            bytes_accessed=48 << 20,
            transcendentals=rows * count * EXPERT_H,
        ),
        name="experts",
    )(tokens, grads, weights, inner, outer)


MESH = pl.DeviceIdType.MESH
SLOW = 4
CHUNKS = 2


def ring_position(index, size):
    fast = size // SLOW
    row, column = lax.div(index, fast), lax.rem(index, fast)
    back = SLOW - 1 - row
    odd = lax.rem(back, 2)
    along = (column - 1) * (1 - odd) + (fast - 1 - column) * odd
    away = lax.div(column + fast - 2, fast - 1)
    return (1 - away) * row + away * (SLOW + back * (fast - 1) + along)


def ring_index(position, size):
    fast = size // SLOW
    away = lax.div(lax.div(position, SLOW) + fast - 2, fast - 1)
    rest = away * (position - SLOW)
    back, step = lax.div(rest, fast - 1), lax.rem(rest, fast - 1)
    odd = lax.rem(back, 2)
    column = (1 + step) * (1 - odd) + (fast - 1 - step) * odd
    return (1 - away) * position * fast + away * ((SLOW - 1 - back) * fast + column)


class Ring:
    def __init__(self, size):
        self.size, self.steps = size, size // 2
        self.me = lax.axis_index("ctx")
        self.place = ring_position(self.me, size)

    def at(self, shift):
        return ring_index(lax.rem(self.place + shift + self.size, self.size), self.size)

    def toward(self, direction, distance):
        return self.at(distance if direction == 0 else -distance)

    def device(self, direction):
        return (self.toward(direction, 1), lax.axis_index("wsh"))

    def meet(self):
        barrier = pltpu.get_barrier_semaphore()
        for direction in range(2):
            pl.semaphore_signal(
                barrier, inc=1, device_id=self.device(direction), device_id_type=MESH
            )
        pl.semaphore_wait(barrier, 2)

    def chunks(self, direction, last):
        if not last:
            return range(CHUNKS)
        half = CHUNKS // 2
        return range(half) if direction == 0 else range(half, CHUNKS)


def rows_at(block, rows, chunk):
    part = rows // CHUNKS
    return pl.ds(pl.multiple_of(block * rows + chunk * part, part), part)


def ring_gather_kernel(size, count, *refs):
    locals_, outs = refs[:count], refs[count : 2 * count]
    send, recv, own = refs[2 * count :]
    ring = Ring(size)
    ring.meet()

    def copy(k, direction, step, chunk, block):
        rows = locals_[k].shape[0]
        source = (
            locals_[k].at[rows_at(0, rows, chunk)]
            if step == 0
            else outs[k].at[rows_at(block, rows, chunk)]
        )
        return pltpu.make_async_remote_copy(
            src_ref=source,
            dst_ref=outs[k].at[rows_at(block, rows, chunk)],
            send_sem=send.at[k, direction, step, chunk],
            recv_sem=recv.at[k, direction, step, chunk],
            device_id=ring.device(direction),
            device_id_type=MESH,
        )

    started = []
    kept = []
    for step in range(ring.steps):
        for chunk in range(CHUNKS):
            for direction in range(2):
                if step > 0:
                    for k in range(count):
                        block = ring.toward(1 - direction, step)
                        copy(k, direction, step - 1, chunk, block).wait_recv()
                if chunk in ring.chunks(direction, step == ring.steps - 1):
                    for k in range(count):
                        moved = copy(k, direction, step, chunk, ring.toward(1 - direction, step))
                        moved.start()
                        started.append(moved)
        if step == 0:
            for k in range(count):
                rows = locals_[k].shape[0]
                place = pl.ds(pl.multiple_of(ring.me * rows, rows), rows)
                kept.append(pltpu.make_async_copy(locals_[k], outs[k].at[place], own.at[k]))
                kept[-1].start()
    last = ring.steps - 1
    for direction in range(2):
        for chunk in ring.chunks(direction, True):
            for k in range(count):
                copy(k, direction, last, chunk, ring.toward(1 - direction, last + 1)).wait_recv()
    for moved in started:
        moved.wait_send()
    for moved in kept:
        moved.wait()


def ring_gather(arrays, size, identity, name):
    count = len(arrays)
    sems = pltpu.SemaphoreType.DMA((count, 2, size // 2, CHUNKS))
    return pl.pallas_call(
        functools.partial(ring_gather_kernel, size, count),
        in_specs=[pl.BlockSpec(memory_space=pltpu.VMEM)] * count,
        out_specs=[pl.BlockSpec(memory_space=pl.ANY)] * count,
        out_shape=[
            jax.ShapeDtypeStruct((size * a.shape[0],) + a.shape[1:], a.dtype) for a in arrays
        ],
        scratch_shapes=[sems, sems, pltpu.SemaphoreType.DMA((count,))],
        compiler_params=pltpu.CompilerParams(collective_id=identity, has_side_effects=True),
        cost_estimate=pl.CostEstimate(flops=0, bytes_accessed=100 << 20, transcendentals=0),
        name=name,
    )(*arrays)


def ring_scatter_kernel(size, count, *refs):
    parts, outs = refs[:count], refs[count : 2 * count]
    stages, lands = refs[2 * count : 3 * count], refs[3 * count : 4 * count]
    send, recv = refs[4 * count :]
    ring = Ring(size)
    ring.meet()

    def copy(k, direction, step, chunk):
        rows = outs[k].shape[0]
        if step == 0:
            source = parts[k].at[rows_at(ring.toward(direction, ring.steps), rows, chunk)]
        else:
            source = stages[k].at[direction, step - 1, rows_at(0, rows, chunk)]
        return pltpu.make_async_remote_copy(
            src_ref=source,
            dst_ref=lands[k].at[direction, step, rows_at(0, rows, chunk)],
            send_sem=send.at[k, direction, step, chunk],
            recv_sem=recv.at[k, direction, step, chunk],
            device_id=ring.device(direction),
            device_id_type=MESH,
        )

    started = []
    for step in range(ring.steps):
        for chunk in range(CHUNKS):
            for direction in range(2):
                for k in range(count):
                    rows = outs[k].shape[0]
                    if step == 0:
                        if chunk not in ring.chunks(direction, True):
                            continue
                    else:
                        here = rows_at(0, rows, chunk)
                        dest = ring.toward(direction, ring.steps - step)
                        total = parts[k][rows_at(dest, rows, chunk)]
                        if step > 1 or chunk in ring.chunks(direction, True):
                            copy(k, direction, step - 1, chunk).wait_recv()
                            landed = lands[k][direction, step - 1, here]
                            total = (total.astype(F32) + landed.astype(F32)).astype(total.dtype)
                        stages[k][direction, step - 1, here] = total
                    moved = copy(k, direction, step, chunk)
                    moved.start()
                    started.append(moved)
    last = ring.steps - 1
    for chunk in range(CHUNKS):
        for k in range(count):
            rows = outs[k].shape[0]
            here = rows_at(0, rows, chunk)
            total = parts[k][rows_at(ring.me, rows, chunk)].astype(F32)
            for direction in range(2):
                copy(k, direction, last, chunk).wait_recv()
                total += lands[k][direction, last, here].astype(F32)
            outs[k][here] = total
    for moved in started:
        moved.wait_send()


def ring_scatter(arrays, size, identity, name):
    count, steps = len(arrays), size // 2
    sems = pltpu.SemaphoreType.DMA((count, 2, steps, CHUNKS))
    blocks = [(a.shape[0] // size,) + a.shape[1:] for a in arrays]
    vmem = pl.BlockSpec(memory_space=pltpu.VMEM)
    return pl.pallas_call(
        functools.partial(ring_scatter_kernel, size, count),
        in_specs=[vmem] * count,
        out_specs=[vmem] * count,
        out_shape=[jax.ShapeDtypeStruct(b, F32) for b in blocks],
        scratch_shapes=[
            pltpu.VMEM((2, steps - 1) + b, a.dtype) for a, b in zip(arrays, blocks)
        ]
        + [pltpu.VMEM((2, steps) + b, a.dtype) for a, b in zip(arrays, blocks)]
        + [sems, sems],
        compiler_params=pltpu.CompilerParams(
            collective_id=identity, has_side_effects=True, vmem_limit_bytes=48 << 20
        ),
        cost_estimate=pl.CostEstimate(flops=0, bytes_accessed=100 << 20, transcendentals=0),
        name=name,
    )(*arrays)


FUSED_BYTES = 52 << 20


def fused_kernel(
    size, x_in, gate_in, g_hbm, wi_hbm, wo_hbm, back_out, gate_out, mix_hbm, dwi_hbm, dwo_hbm,
    x, gates, g, wi, wo, rows, mid, part, gate_part, land, gate_land,
    out_send, out_recv, sum_send, sum_recv, local,
):
    ring = Ring(size)
    steps, me = ring.steps, ring.me
    block, width = x_in.shape
    count = wi.shape[0]
    experts = gate_in.shape[0]
    tile = 256
    loads = [
        pltpu.make_async_copy(a, b, local.at[i])
        for i, (a, b) in enumerate(((wi_hbm, wi), (g_hbm, g), (wo_hbm, wo)))
    ]
    for load in loads:
        load.start()
    ring.meet()
    whole_arrays, own_arrays = (x, gates), (x_in, gate_in)

    def remote(source, target, send, recv, direction):
        return pltpu.make_async_remote_copy(
            src_ref=source,
            dst_ref=target,
            send_sem=send,
            recv_sem=recv,
            device_id=ring.device(direction),
            device_id_type=MESH,
        )

    def spread(k, direction, step, chunk, origin, first=False):
        height = own_arrays[k].shape[0]
        at = rows_at(origin, height, chunk)
        source = own_arrays[k].at[rows_at(0, height, chunk)] if first else whole_arrays[k].at[at]
        return remote(
            source,
            whole_arrays[k].at[at],
            out_send.at[k, direction, step, chunk],
            out_recv.at[k, direction, step, chunk],
            direction,
        )

    for chunk in range(CHUNKS):
        for direction in range(2):
            for k in range(2):
                spread(k, direction, 0, chunk, me, True).start()
    x[pl.ds(pl.multiple_of(me * block, block), block), :] = x_in[...]
    gates[pl.ds(pl.multiple_of(me * experts, experts), experts), :] = gate_in[...]
    for load in loads:
        load.wait()

    lanes = lax.broadcasted_iota(jnp.int32, (block, experts), 1)

    def backward_rows(origin):
        at = pl.ds(pl.multiple_of(origin * block, block), block)
        gate_at = pl.ds(pl.multiple_of(origin * experts, experts), experts)
        turned = gates[gate_at, :].T
        picked = jnp.zeros((block, experts), F32)
        grad = g[at, :]
        for e in range(count):
            mine = lanes == me * count + e
            weight = jnp.sum(jnp.where(mine, turned, 0.0), axis=1, keepdims=True)
            gate_sum = jnp.zeros((block, 1), F32)
            for low in range(0, EXPERT_H, tile):
                gate = dot(x[at, :], wi[e, :, low : low + tile])
                up = dot(x[at, :], wi[e, :, EXPERT_H + low : EXPERT_H + low + tile])
                inward = dot_nt(grad, wo[e, low : low + tile, :])
                sigmoid = 1.0 / (1.0 + jnp.exp(-gate))
                silu = gate * sigmoid
                hidden = (silu * up).astype(BF16).astype(F32)
                gate_sum += jnp.sum(hidden * inward, axis=1, keepdims=True)
                hidden_grad = weight * inward
                to = e * EXPERT_H + low
                mid[at, to : to + tile] = (weight * hidden).astype(BF16)
                to = 2 * e * EXPERT_H + low
                rows[at, to : to + tile] = (
                    hidden_grad * up * sigmoid * (1.0 + gate * (1.0 - sigmoid))
                ).astype(BF16)
                to += EXPERT_H
                rows[at, to : to + tile] = (hidden_grad * silu).astype(BF16)
            picked = jnp.where(mine, gate_sum, picked)
        gate_part[gate_at, :] = picked.T

        @pl.loop(0, width // tile)
        def _(t):
            to = pl.ds(pl.multiple_of(t * tile, tile), tile)
            back = 0.0
            for e in range(count):
                inner = rows[at, 2 * e * EXPERT_H : 2 * (e + 1) * EXPERT_H]
                back += dot_nt(inner, wi[e, to, :])
            part[at, to] = back.astype(BF16)

    def visit(j, carry):
        step = lax.div(j + 1, 2)
        odd = lax.rem(j, 2)

        @pl.when((odd == 1) & (j < size - 1))
        def _():
            for chunk in range(CHUNKS):
                for direction in range(2):
                    origin = ring.toward(1 - direction, step)
                    for k in range(2):
                        spread(k, direction, step - 1, chunk, origin).wait_recv()

                    def forward():
                        for k in range(2):
                            spread(k, direction, step, chunk, origin).start()

                    if chunk in ring.chunks(direction, True):
                        forward()
                    else:
                        pl.when(step < steps - 1)(forward)

        @pl.when(j == size - 1)
        def _():
            for direction in range(2):
                for chunk in ring.chunks(direction, True):
                    for k in range(2):
                        origin = ring.toward(1 - direction, steps)
                        spread(k, direction, steps - 1, chunk, origin).wait_recv()

        backward_rows(ring.at(step * (1 - 2 * odd)))
        return carry

    lax.fori_loop(0, size, visit, 0)

    parts, lands, outs = (part, gate_part), (land, gate_land), (back_out, gate_out)

    def inward_copy(k, direction, step, chunk):
        height = own_arrays[k].shape[0]
        dest = ring.toward(direction, steps - step)
        return remote(
            parts[k].at[rows_at(dest, height, chunk)],
            lands[k].at[direction, step, rows_at(0, height, chunk)],
            sum_send.at[k, direction, step, chunk],
            sum_recv.at[k, direction, step, chunk],
            direction,
        )

    def inward_step(step):
        for chunk in range(CHUNKS):
            for direction in range(2):
                near = chunk in ring.chunks(direction, True)
                if step == 0 and not near:
                    continue
                for k in range(2):
                    height = own_arrays[k].shape[0]
                    if step > 1 or (step == 1 and near):
                        inward_copy(k, direction, step - 1, chunk).wait_recv()
                        at = rows_at(ring.toward(direction, steps - step), height, chunk)
                        landed = lands[k][direction, step - 1, rows_at(0, height, chunk)]
                        both = parts[k][at, :].astype(F32) + landed.astype(F32)
                        parts[k][at, :] = both.astype(parts[k].dtype)
                    inward_copy(k, direction, step, chunk).start()

    def inner_gradient(t):
        to = pl.ds(pl.multiple_of(t * tile, tile), tile)
        for e in range(count):
            inner = rows[:, 2 * e * EXPERT_H : 2 * (e + 1) * EXPERT_H]
            wi[e, to, :] = dot_tn(x[:, to], inner).astype(BF16)

    def outer_gradient(t):
        e = lax.div(t, EXPERT_H // tile)
        low = lax.rem(t, EXPERT_H // tile)
        from_ = pl.ds(pl.multiple_of(t * tile, tile), tile)
        to = pl.ds(pl.multiple_of(low * tile, tile), tile)
        wo[e, to, :] = dot_tn(mid[:, from_], g[...]).astype(BF16)

    def mixture(origin):
        at = pl.ds(pl.multiple_of(origin * block, block), block)
        mixed = 0.0
        for e in range(count):
            mixed += dot(mid[at, e * EXPERT_H : (e + 1) * EXPERT_H], wo[e])
        x[at, :] = mixed.astype(BF16)

    tiles = width // tile
    cuts = [round(tiles * i / (steps - 1)) for i in range(steps)]
    stores = [
        pltpu.make_async_copy(a, b, local.at[i])
        for i, (a, b) in enumerate(((wi, dwi_hbm), (x, mix_hbm), (wo, dwo_hbm)))
    ]
    for step in range(steps):
        inward_step(step)
        if step < steps - 1:
            pl.loop(cuts[step], cuts[step + 1])(inner_gradient)
        else:
            stores[0].start()
            for k in range(2):
                for direction in range(2):
                    for hop in range(steps):
                        for chunk in ring.chunks(direction, hop == steps - 1):
                            spread(k, direction, hop, chunk, me, hop == 0).wait_send()
            pl.loop(0, size)(mixture)
            stores[1].start()
            pl.loop(0, count * EXPERT_H // tile)(outer_gradient)
            stores[2].start()
    for chunk in range(CHUNKS):
        for k in range(2):
            height = own_arrays[k].shape[0]
            here = rows_at(0, height, chunk)
            total = parts[k][rows_at(me, height, chunk), :].astype(F32)
            for direction in range(2):
                inward_copy(k, direction, steps - 1, chunk).wait_recv()
                total += lands[k][direction, steps - 1, here].astype(F32)
            outs[k][here, :] = total
    for k in range(2):
        for direction in range(2):
            for step in range(steps):
                for chunk in ring.chunks(direction, step == 0):
                    inward_copy(k, direction, step, chunk).wait_send()
    for store in stores:
        store.wait()


def fused_scratch(tokens, gates, inner, outer, size):
    block, width = tokens.shape
    count, steps = inner.shape[0], size // 2
    rows, gate_rows = size * block, size * gates.shape[0]
    return [
        pltpu.VMEM((rows, width), BF16),
        pltpu.VMEM((gate_rows, block), F32),
        pltpu.VMEM((rows, width), BF16),
        pltpu.VMEM(inner.shape, BF16),
        pltpu.VMEM(outer.shape, BF16),
        pltpu.VMEM((rows, 2 * count * EXPERT_H), BF16),
        pltpu.VMEM((rows, count * EXPERT_H), BF16),
        pltpu.VMEM((rows, width), BF16),
        pltpu.VMEM((gate_rows, block), F32),
        pltpu.VMEM((2, steps, block, width), BF16),
        pltpu.VMEM((2, steps) + gates.shape, F32),
    ]


def fused_fits(*shapes):
    return sum(r.dtype.itemsize * functools.reduce(lambda a, b: a * b, r.shape) for r in fused_scratch(*shapes)) <= FUSED_BYTES


def fused_experts(tokens, gates, grads, inner, outer, size, identity):
    block, width = tokens.shape
    count, steps = inner.shape[0], size // 2
    rows = size * block
    vmem, hbm = pl.BlockSpec(memory_space=pltpu.VMEM), pl.BlockSpec(memory_space=pl.ANY)
    sems = pltpu.SemaphoreType.DMA((2, 2, steps, CHUNKS))
    return pl.pallas_call(
        functools.partial(fused_kernel, size),
        in_specs=[vmem, vmem, hbm, hbm, hbm],
        out_specs=[vmem, vmem, hbm, hbm, hbm],
        out_shape=[
            jax.ShapeDtypeStruct(tokens.shape, F32),
            jax.ShapeDtypeStruct(gates.shape, F32),
            jax.ShapeDtypeStruct((rows, width), BF16),
            jax.ShapeDtypeStruct(inner.shape, BF16),
            jax.ShapeDtypeStruct(outer.shape, BF16),
        ],
        scratch_shapes=fused_scratch(tokens, gates, inner, outer, size)
        + [sems] * 4
        + [pltpu.SemaphoreType.DMA((3,))],
        compiler_params=pltpu.CompilerParams(
            collective_id=identity, has_side_effects=True, vmem_limit_bytes=63 << 20
        ),
        cost_estimate=pl.CostEstimate(
            flops=18 * count * rows * width * EXPERT_H,
            bytes_accessed=300 << 20,
            transcendentals=rows * count * EXPERT_H,
        ),
        name="fused_experts",
    )(tokens, gates, grads, inner, outer)


EXTRA = 16


def reduce_kernel(
    size, shards, lhs, rhs, small, out, part, cores, lines, total, stage, land, held,
    core_send, core_recv, line_send, line_recv, ring_send, ring_recv, all_send, all_recv,
):
    ring = Ring(size)
    steps, height = ring.steps, shards // 2
    spot = lax.axis_index("wsh")
    core, row = lax.rem(spot, 2), lax.div(spot, 2)
    ctx = ring.me
    slot_rows, width = total.shape[1], total.shape[2]
    shard_rows = slot_rows - EXTRA
    split = width // CHUNKS
    mate = (ctx, row * 2 + 1 - core)
    above = (ctx, lax.rem(row + 1, height) * 2 + core)
    below = (ctx, lax.rem(row + height - 1, height) * 2 + core)

    barrier = pltpu.get_barrier_semaphore()
    for device in (mate, above, below, ring.device(0), ring.device(1)):
        pl.semaphore_signal(barrier, inc=1, device_id=device, device_id_type=MESH)
    pl.semaphore_wait(barrier, 5)

    order = [steps]
    for distance in range(steps - 1, 0, -1):
        order += [distance, -distance]
    order.append(0)
    slot_of = {shift: i for i, shift in enumerate(order)}
    slot_of[-steps] = 0
    blocks = [ring.at(shift) for shift in order]
    started = []

    def begin(copy):
        copy.start()
        started.append(copy)

    def remote(source, target, send, recv, device):
        return pltpu.make_async_remote_copy(
            src_ref=source,
            dst_ref=target,
            send_sem=send,
            recv_sem=recv,
            device_id=device,
            device_id_type=MESH,
        )

    def to_mate(i, y):
        return remote(
            part.at[i, y * 2 + 1 - core], cores.at[i, y], core_send.at[i, y], core_recv.at[i, y], mate
        )

    def to_line(i, t):
        shard = lax.rem(row + 2 * height - 1 - t, height) * 2 + core
        return remote(
            part.at[i, shard], lines.at[i, t], line_send.at[i, t], line_recv.at[i, t], above
        )

    def form(i):
        at = pl.multiple_of(blocks[i] * width, width)
        side = lax.div(blocks[i] * width, lhs.shape[1] + 2 * KEY_HEADS * HEAD_SIZE)

        @pl.loop(0, shards)
        def _(w):
            rows = pl.ds(pl.multiple_of(w * shard_rows, shard_rows), shard_rows)
            product = dot(lhs[side, rows, :], rhs[:, pl.ds(at, width)])
            part[i, w, :shard_rows, :] = product.astype(BF16)
            part[i, w, shard_rows:, :] = small[w, :, pl.ds(at, width)]

        for y in range(height):
            begin(to_mate(i, y))

    def add_cores(i):
        for y in range(height):
            to_mate(i, y).wait_recv()
            both = part[i, y * 2 + core].astype(F32) + cores[i, y].astype(F32)
            part[i, y * 2 + core] = both.astype(BF16)
        begin(to_line(i, 0))

    for i in range(size):
        form(i)
        if i > 0:
            add_cores(i - 1)
    add_cores(size - 1)
    for t in range(1, height - 1):
        for i in range(size):
            to_line(i, t - 1).wait_recv()
            shard = lax.rem(row + 2 * height - 1 - t, height) * 2 + core
            both = part[i, shard].astype(F32) + lines[i, t - 1].astype(F32)
            part[i, shard] = both.astype(BF16)
            begin(to_line(i, t))

    def finish_line(i):
        to_line(i, height - 2).wait_recv()
        total[i] = part[i, spot].astype(F32) + lines[i, height - 2].astype(F32)

    def columns(chunk):
        return pl.ds(chunk * split, split)

    def around(direction, step, chunk):
        return remote(
            stage.at[direction, step, :, columns(chunk)],
            land.at[direction, step, :, columns(chunk)],
            ring_send.at[direction, step, chunk],
            ring_recv.at[direction, step, chunk],
            ring.device(direction),
        )

    for step in range(steps):
        reach = steps - step
        for i in sorted({slot_of[reach], slot_of[-reach]}):
            finish_line(i)
        for chunk in range(CHUNKS):
            for direction in range(2):
                if step == 0 and chunk not in ring.chunks(direction, True):
                    continue
                at = columns(chunk)
                value = total[slot_of[reach if direction == 0 else -reach], :, at]
                if step > 1 or (step == 1 and chunk in ring.chunks(direction, True)):
                    around(direction, step - 1, chunk).wait_recv()
                    value += land[direction, step - 1, :, at].astype(F32)
                stage[direction, step, :, at] = value.astype(BF16)
                begin(around(direction, step, chunk))

    def onward(direction, step, chunk, block):
        return remote(
            held.at[block, :, columns(chunk)],
            held.at[block, :, columns(chunk)],
            all_send.at[direction, step, chunk],
            all_recv.at[direction, step, chunk],
            ring.device(direction),
        )

    def put(block, chunk):
        at = pl.ds(pl.multiple_of(block * width + chunk * split, split), split)
        out[:, at] = held[block, :, columns(chunk)].astype(F32)

    own = slot_of[0]
    finish_line(own)
    for chunk in range(CHUNKS):
        at = columns(chunk)
        value = total[own, :, at]
        for direction in range(2):
            around(direction, steps - 1, chunk).wait_recv()
            value += land[direction, steps - 1, :, at].astype(F32)
        held[ctx, :, at] = value.astype(BF16)
        for direction in range(2):
            begin(onward(direction, 0, chunk, ctx))
    for chunk in range(CHUNKS):
        put(ctx, chunk)
    for step in range(1, steps + 1):
        for chunk in range(CHUNKS):
            for direction in range(2):
                if step == steps and chunk not in ring.chunks(direction, True):
                    continue
                block = ring.toward(1 - direction, step)
                onward(direction, step - 1, chunk, block).wait_recv()
                if step < steps and chunk in ring.chunks(direction, step == steps - 1):
                    begin(onward(direction, step, chunk, block))
                put(block, chunk)
    for copy in started:
        copy.wait_send()


def reduce_grads(lhs, rhs, small, size, shards, identity):
    steps, height = size // 2, shards // 2
    columns = rhs.shape[1]
    width, rows = columns // size, lhs.shape[1] // shards + EXTRA
    vmem = pl.BlockSpec(memory_space=pltpu.VMEM)
    dma = pltpu.SemaphoreType.DMA
    return pl.pallas_call(
        functools.partial(reduce_kernel, size, shards),
        in_specs=[vmem] * 3,
        out_specs=vmem,
        out_shape=jax.ShapeDtypeStruct((rows, columns), F32),
        scratch_shapes=[
            pltpu.VMEM((size, shards, rows, width), BF16),
            pltpu.VMEM((size, height, rows, width), BF16),
            pltpu.VMEM((size, height - 1, rows, width), BF16),
            pltpu.VMEM((size, rows, width), F32),
            pltpu.VMEM((2, steps, rows, width), BF16),
            pltpu.VMEM((2, steps, rows, width), BF16),
            pltpu.VMEM((size, rows, width), BF16),
            dma((size, height)),
            dma((size, height)),
            dma((size, height - 1)),
            dma((size, height - 1)),
        ]
        + [dma((2, steps, CHUNKS))] * 4,
        compiler_params=pltpu.CompilerParams(
            collective_id=identity, has_side_effects=True, vmem_limit_bytes=62 << 20
        ),
        cost_estimate=pl.CostEstimate(
            flops=2 * lhs.shape[1] * lhs.shape[2] * columns,
            bytes_accessed=300 << 20,
            transcendentals=0,
        ),
        name="reduce_grads",
    )(lhs, rhs, small)


def on_device(
    layer_input,
    attention_gain,
    query_weight,
    key_matrix,
    value_matrix,
    output_weight,
    expert_gain,
    router_weight,
    expert_inner,
    expert_outer,
    document_lengths,
    token_places,
    expert_routes,
    cotangent,
):
    group_devices = lax.axis_size("ctx")
    ctx_index = lax.axis_index("ctx")
    token_rows = layer_input.shape[1]
    experts = router_weight.shape[1]
    own_experts = expert_inner.shape[0]
    key_value_width = KEY_HEADS * HEAD_SIZE

    def gather(shard, axis=0):
        return lax.all_gather(shard, "wsh", axis=axis, tiled=True)

    projected = 2 * key_value_width + query_weight.shape[1]
    small = jnp.concatenate([attention_gain[:, None], expert_gain[:, None], router_weight], axis=1)
    small = jnp.pad(small, ((0, 0), (0, -small.shape[1] % 128)))
    first_weights = gather(
        jnp.concatenate([query_weight, key_matrix, value_matrix, small], axis=1)
    )
    whole_qkv = first_weights[:, :projected]
    gain_one = first_weights[:, projected].astype(F32)
    gain_two = first_weights[:, projected + 1].astype(F32)
    whole_router = first_weights[:, projected + 2 : projected + 2 + experts]
    whole_output = gather(output_weight)
    whole_inner = gather(expert_inner, 1)
    whole_outer = gather(expert_outer, 1)
    (all_grads,) = ring_gather([cotangent[0]], group_devices, 6, "gather_grads")

    places_all = token_places[0]
    key_documents, key_offsets = locate(document_lengths[0], places_all)
    first_row = ctx_index * token_rows
    query_places = lax.dynamic_slice_in_dim(places_all, first_row, token_rows)
    query_documents = lax.dynamic_slice_in_dim(key_documents, first_row, token_rows)
    query_offsets = lax.dynamic_slice_in_dim(key_offsets, first_row, token_rows)
    marks = (
        key_documents[:, None],
        places_all[:, None],
        query_documents[None, :],
        query_places[None, :],
    )
    cosine_rows, sine_table = angles_for(query_offsets)

    own_input, all_grads = lax.optimization_barrier((layer_input[0], all_grads))
    inputs_f = own_input.astype(F32)
    inverse_one = rms_inverse(inputs_f)
    normed_one = (inputs_f * inverse_one * gain_one).astype(BF16)
    pre = dot(normed_one, whole_qkv)
    query_pre = pre[:, : -2 * key_value_width]
    key_pre = pre[:, -2 * key_value_width : -key_value_width]
    keys = (
        apply_rotation(key_pre.reshape(token_rows, KEY_HEADS, HEAD_SIZE), cosine_rows, sine_table)
        .astype(BF16)
        .reshape(token_rows, key_value_width)
    )
    values = pre[:, -key_value_width:].astype(BF16)
    all_keys, all_values = ring_gather([keys, values], group_devices, 1, "gather_keys")
    queries = (
        apply_rotation(
            query_pre.reshape(token_rows, QUERY_HEADS, HEAD_SIZE), cosine_rows, sine_table
        ).astype(BF16)
        * SCALE
    ).reshape(token_rows, QUERY_HEADS * HEAD_SIZE)
    spread_queries = spread_heads(queries)
    spread_attended, lse = attend(spread_queries, all_keys, all_values, marks)
    attended_f = gather_heads(spread_attended)
    attended = attended_f.astype(BF16)
    residual = inputs_f + dot(attended, whole_output)
    inverse_two = rms_inverse(residual)
    normed_two = (residual * inverse_two * gain_two).astype(BF16)
    logits = dot(normed_two, whole_router)
    expert_ids = jnp.arange(experts, dtype=jnp.int32)
    routed = jnp.any(expert_routes[0][:, :, None] == expert_ids[None, None, :], axis=1)
    gates = jax.nn.softmax(jnp.where(routed, logits, -jnp.inf), axis=-1)

    turned_gates = gates.T
    if fused_fits(normed_two, turned_gates, whole_inner, whole_outer, group_devices):
        back_sum, gate_grad, mixed, inner_grad, outer_grad = fused_experts(
            normed_two, turned_gates, all_grads, whole_inner, whole_outer, group_devices, 7
        )
    else:
        all_tokens, all_gates = ring_gather([normed_two, turned_gates], group_devices, 2, "gather_tokens")
        own_gates = (
            lax.dynamic_slice_in_dim(
                all_gates.reshape(group_devices, experts, token_rows),
                ctx_index * own_experts,
                own_experts,
                axis=1,
            )
            .transpose(0, 2, 1)
            .reshape(group_devices * token_rows, own_experts)
        )
        mixed, back_rows, own_gate_grad, inner_grad, outer_grad = experts_pass(
            all_tokens, all_grads, own_gates, whole_inner, whole_outer
        )
        placed = lax.dynamic_update_slice_in_dim(
            jnp.zeros((group_devices, experts, token_rows), F32),
            own_gate_grad.reshape(group_devices, token_rows, own_experts).transpose(0, 2, 1),
            ctx_index * own_experts,
            axis=1,
        ).reshape(group_devices * experts, token_rows)
        back_sum, gate_grad = ring_scatter([back_rows, placed], group_devices, 3, "scatter_rows")
    gate_grad = gate_grad.T
    out_grad = cotangent[0].astype(F32)
    logit_grad = (
        gates * (gate_grad - jnp.sum(gates * gate_grad, axis=-1, keepdims=True))
    ).astype(BF16)
    router_grad = dot_tn(normed_two, logit_grad)
    normed_two_grad = dot_nt(logit_grad, whole_router) + back_sum
    gain_two_grad, residual_back = norm_backward(residual, inverse_two, gain_two, normed_two_grad)
    residual_grad = out_grad + residual_back
    branch_grad = residual_grad.astype(BF16)
    attended_grad = dot_nt(branch_grad, whole_output).astype(BF16)
    delta = jnp.sum(
        (attended_grad.astype(F32) * attended_f).reshape(token_rows, QUERY_HEADS, HEAD_SIZE), axis=-1
    ).T.reshape(PAIRS, PAIR_HEADS, 1, token_rows)
    spread_grads = spread_heads(attended_grad)
    spread_query_grad, key_part, value_part = attend_back(
        spread_queries,
        spread_queries.transpose(0, 1, 3, 2),
        spread_grads,
        spread_grads.transpose(0, 1, 3, 2),
        all_keys,
        all_values,
        lse,
        delta,
        marks,
    )
    key_grad, value_grad = ring_scatter([key_part, value_part], group_devices, 4, "scatter_keys")
    value_grad = value_grad.astype(BF16)
    query_pre_grad = (
        reverse_rotation(
            (gather_heads(spread_query_grad) * SCALE).reshape(token_rows, QUERY_HEADS, HEAD_SIZE),
            cosine_rows,
            sine_table,
        )
        .reshape(token_rows, QUERY_HEADS * HEAD_SIZE)
        .astype(BF16)
    )
    key_pre_grad = (
        reverse_rotation(
            key_grad.reshape(token_rows, KEY_HEADS, HEAD_SIZE), cosine_rows, sine_table
        )
        .reshape(token_rows, key_value_width)
        .astype(BF16)
    )
    pre_grad = jnp.concatenate([query_pre_grad, key_pre_grad, value_grad], axis=1)
    normed_one_grad = dot_nt(pre_grad, whole_qkv)
    gain_one_grad, input_back = norm_backward(inputs_f, inverse_one, gain_one, normed_one_grad)
    input_grad = residual_grad + input_back

    def scatter(grad, dim=0):
        return lax.psum_scatter(grad.astype(BF16), "wsh", scatter_dimension=dim, tiled=True)

    inner_out = scatter(inner_grad, 1)
    outer_out = scatter(outer_grad, 1)
    mixed, inner_out, outer_out = lax.optimization_barrier((mixed, inner_out, outer_out))
    mixture = lax.psum_scatter(mixed, "ctx", scatter_dimension=0, tiled=True)
    shards = lax.axis_size("wsh")
    shard_rows = query_weight.shape[0]
    columns = 2 * query_weight.shape[1] + 2 * key_value_width
    marks_small = jnp.concatenate(
        [gain_one_grad[None], gain_two_grad[None], router_grad.T], axis=0
    ).astype(BF16)
    small_count = marks_small.shape[0]
    small_rows = marks_small.reshape(small_count, shards, shard_rows).transpose(1, 0, 2)
    small_rows = small_rows.reshape(shards, small_count * shard_rows)
    across = -(-small_count * shard_rows // EXTRA // 128) * 128
    small_rows = jnp.pad(small_rows, ((0, 0), (0, EXTRA * across - small_rows.shape[1])))
    small_rows = jnp.pad(
        small_rows.reshape(shards, EXTRA, across), ((0, 0), (0, 0), (0, columns - across))
    )
    summed = reduce_grads(
        jnp.stack([normed_one.T, attended.T]),
        jnp.concatenate([pre_grad, branch_grad], axis=1),
        small_rows,
        group_devices,
        shards,
        5,
    )
    mixture, summed = lax.optimization_barrier((mixture, summed))
    layer_output = (residual + mixture.astype(F32)).astype(BF16)
    small_out = summed[shard_rows:, :across].reshape(-1)[: small_count * shard_rows]
    small_out = small_out.reshape(small_count, shard_rows)
    ends = [0]
    for shard in (query_weight, key_matrix, value_matrix, output_weight):
        ends.append(ends[-1] + shard.shape[1])
    query_out, key_out, value_out, output_out = (
        summed[:shard_rows, start:end] for start, end in zip(ends, ends[1:])
    )
    return (
        layer_output[None],
        input_grad[None],
        small_out[0],
        query_out,
        key_out,
        value_out,
        output_out,
        small_out[1],
        small_out[2:].T,
        inner_out.astype(F32),
        outer_out.astype(F32),
    )


def solution(mesh):
    tokens = P("wsh", "ctx", None)
    shard, expert = P("wsh", None), P("ctx", "wsh", None)
    return jax.shard_map(
        on_device,
        mesh=mesh,
        in_specs=(
            tokens,
            P("wsh"),
            shard,
            shard,
            shard,
            shard,
            P("wsh"),
            shard,
            expert,
            expert,
            shard,
            shard,
            tokens,
            tokens,
        ),
        out_specs=(
            tokens,
            tokens,
            P("wsh"),
            shard,
            shard,
            shard,
            shard,
            P("wsh"),
            shard,
            expert,
            expert,
        ),
        check_vma=False,
    )
```

```python
import functools

import jax
import jax.numpy as jnp
from jax import lax
from jax.experimental import pallas as pl
from jax.experimental.pallas import tpu as pltpu
from jax.sharding import PartitionSpec as P

QUERY_HEADS = 24
KEY_HEADS = 8
HEAD_SIZE = 64
EXPERT_H = 512
TOPK = 8
SEQS = 4
GROUP = QUERY_HEADS // KEY_HEADS
PAIRS = KEY_HEADS // 2
PAIR_HEADS = 2 * GROUP
PAIR_WIDTH = 2 * HEAD_SIZE

EPS = 1e-05
THETA = 10000.0
MASK_FILL = -1e30
SCALE = HEAD_SIZE**-0.5
BF16 = jnp.bfloat16
F32 = jnp.float32


def dot(a, b):
    return jnp.dot(a, b, preferred_element_type=F32)


def dot_nt(a, b):
    return lax.dot_general(a, b, (((1,), (1,)), ((), ())), preferred_element_type=F32)


def dot_tn(a, b):
    return lax.dot_general(a, b, (((0,), (0,)), ((), ())), preferred_element_type=F32)


def rms_inverse(matrix):
    return lax.rsqrt(jnp.mean(matrix * matrix, axis=-1, keepdims=True) + EPS)


def locate(lengths_row, places_row):
    segment_ends = jnp.cumsum(lengths_row)
    beyond = (places_row[:, None] >= segment_ends[None, :]).astype(jnp.int32)
    documents = jnp.sum(beyond, axis=1)
    offsets = places_row - jnp.sum(beyond * lengths_row[None, :], axis=1)
    return (documents, offsets)


def angles_for(offsets):
    halfway = HEAD_SIZE // 2
    frequency = THETA ** (-2.0 * jnp.arange(halfway, dtype=F32) / HEAD_SIZE)
    angles = offsets.astype(F32)[:, None] * frequency[None, :]
    return (jnp.cos(angles)[:, None, :], jnp.sin(angles)[:, None, :])


def apply_rotation(matrix, cosine_rows, sine_table):
    halfway = matrix.shape[-1] // 2
    former = matrix[..., :halfway]
    latter = matrix[..., halfway:]
    return jnp.concatenate(
        [former * cosine_rows - latter * sine_table, latter * cosine_rows + former * sine_table],
        axis=-1,
    )


def reverse_rotation(matrix, cosine_rows, sine_table):
    return apply_rotation(matrix, cosine_rows, -sine_table)


def norm_backward(matrix, inverse, gains, gradients):
    scaled = gradients * gains
    gain_grad = jnp.sum(gradients * matrix * inverse, axis=0)
    input_back = inverse * scaled - matrix * inverse * inverse * inverse * jnp.mean(
        scaled * matrix, axis=-1, keepdims=True
    )
    return (gain_grad, input_back)


def spread_heads(rows):
    tokens = rows.shape[0]
    heads = rows.reshape(tokens, PAIRS, 2, GROUP, HEAD_SIZE).transpose(1, 2, 3, 4, 0)
    zero = jnp.zeros_like(heads[:, 0])
    low = jnp.concatenate([heads[:, 0], zero], axis=2)
    high = jnp.concatenate([zero, heads[:, 1]], axis=2)
    return jnp.stack([low, high], axis=1).reshape(PAIRS, PAIR_HEADS, PAIR_WIDTH, tokens)


def gather_heads(spread):
    tokens = spread.shape[-1]
    split = spread.reshape(PAIRS, 2, GROUP, 2, HEAD_SIZE, tokens)
    heads = jnp.stack([split[:, 0, :, 0], split[:, 1, :, 1]], axis=1)
    return heads.transpose(4, 0, 1, 2, 3).reshape(tokens, QUERY_HEADS * HEAD_SIZE)


def fill_bias(bias_ref, kdoc_ref, kplace_ref, qdoc_ref, qplace_ref):
    kdoc, kplace = kdoc_ref[...], kplace_ref[...]
    qdoc, qplace = qdoc_ref[...], qplace_ref[...]
    seen = (kdoc == qdoc) & (qdoc < SEQS) & (kplace <= qplace) | (kplace == qplace)
    bias_ref[...] = jnp.where(seen, 0.0, MASK_FILL)


def attend_kernel(
    q_ref, k_ref, v_ref, kdoc_ref, kplace_ref, qdoc_ref, qplace_ref, o_ref, lse_ref, bias, vt
):
    pair, head = pl.program_id(0), pl.program_id(1)

    @pl.when((pair == 0) & (head == 0))
    def _():
        fill_bias(bias, kdoc_ref, kplace_ref, qdoc_ref, qplace_ref)

    @pl.when(head == 0)
    def _():
        vt[...] = v_ref[...].T

    scores = dot(k_ref[...], q_ref[0, 0]) + bias[...]
    top = jnp.max(scores, axis=0, keepdims=True)
    weights = jnp.exp(scores - top)
    total = jnp.sum(weights, axis=0, keepdims=True)
    o_ref[0, 0] = dot(vt[...], weights.astype(BF16)) / total
    lse_ref[0, 0] = top + jnp.log(total)


def attend_back_kernel(
    q_ref,
    qt_ref,
    g_ref,
    gt_ref,
    k_ref,
    v_ref,
    lse_ref,
    delta_ref,
    kdoc_ref,
    kplace_ref,
    qdoc_ref,
    qplace_ref,
    dq_ref,
    dk_ref,
    dv_ref,
    bias,
    kt,
    dk_sum,
    dv_sum,
):
    pair, head = pl.program_id(0), pl.program_id(1)

    @pl.when((pair == 0) & (head == 0))
    def _():
        fill_bias(bias, kdoc_ref, kplace_ref, qdoc_ref, qplace_ref)

    @pl.when(head == 0)
    def _():
        kt[...] = k_ref[...].T
        dk_sum[...] = jnp.zeros_like(dk_sum)
        dv_sum[...] = jnp.zeros_like(dv_sum)

    scores = dot(k_ref[...], q_ref[0, 0]) + bias[...]
    probs = jnp.exp(scores - lse_ref[0, 0])
    prob_grad = dot(v_ref[...], g_ref[0, 0])
    score_grad = (probs * (prob_grad - delta_ref[0, 0])).astype(BF16)
    dv_sum[...] += dot(probs.astype(BF16), gt_ref[0, 0])
    dk_sum[...] += dot(score_grad, qt_ref[0, 0])
    dq_ref[0, 0] = dot(kt[...], score_grad)

    @pl.when(head == PAIR_HEADS - 1)
    def _():
        dk_ref[...] = dk_sum[...].astype(BF16)
        dv_ref[...] = dv_sum[...].astype(BF16)


def whole(shape):
    return pl.BlockSpec(shape, lambda *_: (0,) * len(shape))


def attention_specs(tokens, rows):
    head = pl.BlockSpec((1, 1, PAIR_WIDTH, tokens), lambda p, h: (p, h, 0, 0))
    head_t = pl.BlockSpec((1, 1, tokens, PAIR_WIDTH), lambda p, h: (p, h, 0, 0))
    line = pl.BlockSpec((1, 1, 1, tokens), lambda p, h: (p, h, 0, 0))
    keys = pl.BlockSpec((rows, PAIR_WIDTH), lambda p, h: (0, p))
    marks = [whole((rows, 1)), whole((rows, 1)), whole((1, tokens)), whole((1, tokens))]
    return head, head_t, line, keys, marks


def attend(queries, keys, values, marks):
    tokens, rows = queries.shape[-1], keys.shape[0]
    head, _, line, key_spec, mark_specs = attention_specs(tokens, rows)
    return pl.pallas_call(
        attend_kernel,
        grid=(PAIRS, PAIR_HEADS),
        in_specs=[head, key_spec, key_spec] + mark_specs,
        out_specs=[head, line],
        out_shape=[
            jax.ShapeDtypeStruct((PAIRS, PAIR_HEADS, PAIR_WIDTH, tokens), F32),
            jax.ShapeDtypeStruct((PAIRS, PAIR_HEADS, 1, tokens), F32),
        ],
        scratch_shapes=[pltpu.VMEM((rows, tokens), F32), pltpu.VMEM((PAIR_WIDTH, rows), BF16)],
        cost_estimate=pl.CostEstimate(
            flops=4 * QUERY_HEADS * tokens * rows * PAIR_WIDTH,
            bytes_accessed=16 << 20,
            transcendentals=QUERY_HEADS * tokens * rows,
        ),
        name="attend",
    )(queries, keys, values, *marks)


def attend_back(queries, queries_t, grads, grads_t, keys, values, lse, delta, marks):
    tokens, rows = queries.shape[-1], keys.shape[0]
    head, head_t, line, key_spec, mark_specs = attention_specs(tokens, rows)
    return pl.pallas_call(
        attend_back_kernel,
        grid=(PAIRS, PAIR_HEADS),
        in_specs=[head, head_t, head, head_t, key_spec, key_spec, line, line] + mark_specs,
        out_specs=[head, key_spec, key_spec],
        out_shape=[
            jax.ShapeDtypeStruct((PAIRS, PAIR_HEADS, PAIR_WIDTH, tokens), F32),
            jax.ShapeDtypeStruct(keys.shape, BF16),
            jax.ShapeDtypeStruct(keys.shape, BF16),
        ],
        scratch_shapes=[
            pltpu.VMEM((rows, tokens), F32),
            pltpu.VMEM((PAIR_WIDTH, rows), BF16),
            pltpu.VMEM((rows, PAIR_WIDTH), F32),
            pltpu.VMEM((rows, PAIR_WIDTH), F32),
        ],
        cost_estimate=pl.CostEstimate(
            flops=10 * QUERY_HEADS * tokens * rows * PAIR_WIDTH,
            bytes_accessed=24 << 20,
            transcendentals=QUERY_HEADS * tokens * rows,
        ),
        name="attend_back",
    )(queries, queries_t, grads, grads_t, keys, values, lse, delta, *marks)


def expert_kernel(
    x_ref, g_ref, w_ref, wi_ref, wo_ref, mix_ref, back_ref, gate_ref, dwi_ref, dwo_ref, dwi, dwo, mid, rows
):
    step = pl.program_id(0)
    count, width = wi_ref.shape[0], wi_ref.shape[1]

    @pl.when(step == 0)
    def _():
        dwi[...] = jnp.zeros_like(dwi)
        dwo[...] = jnp.zeros_like(dwo)

    grad = g_ref[...]
    for e in range(count):
        gate_up = dot(x_ref[...], wi_ref[e])
        gate, up = gate_up[:, :EXPERT_H], gate_up[:, EXPERT_H:]
        sigmoid = 1.0 / (1.0 + jnp.exp(-gate))
        silu = gate * sigmoid
        hidden = (silu * up).astype(BF16).astype(F32)
        weight = w_ref[:, e : e + 1]
        inward = dot_nt(grad, wo_ref[e])
        gate_ref[:, e : e + 1] = jnp.sum(hidden * inward, axis=1, keepdims=True)
        weighted = (weight * hidden).astype(BF16)
        hidden_grad = weight * inward
        mid[:, e * EXPERT_H : (e + 1) * EXPERT_H] = weighted
        at = 2 * e * EXPERT_H
        rows[:, at : at + EXPERT_H] = (
            hidden_grad * up * sigmoid * (1.0 + gate * (1.0 - sigmoid))
        ).astype(BF16)
        rows[:, at + EXPERT_H : at + 2 * EXPERT_H] = (hidden_grad * silu).astype(BF16)
        dwo[e] += dot_tn(weighted, grad)
    tile = 256
    for e in range(count):
        inner = rows[:, 2 * e * EXPERT_H : 2 * (e + 1) * EXPERT_H]

        @pl.loop(0, width // tile)
        def _(t):
            at = pl.multiple_of(t * tile, tile)
            dwi[e, pl.ds(at, tile), :] += dot_tn(x_ref[:, pl.ds(at, tile)], inner)

    @pl.loop(0, width // tile)
    def _(t):
        at = pl.multiple_of(t * tile, tile)
        mixed, back = 0.0, 0.0
        for e in range(count):
            mixed += dot(mid[:, e * EXPERT_H : (e + 1) * EXPERT_H], wo_ref[e, :, pl.ds(at, tile)])
            back += dot_nt(
                rows[:, 2 * e * EXPERT_H : 2 * (e + 1) * EXPERT_H], wi_ref[e, pl.ds(at, tile), :]
            )
        mix_ref[:, pl.ds(at, tile)] = mixed.astype(BF16)
        back_ref[:, pl.ds(at, tile)] = back.astype(BF16)

    @pl.when(step == pl.num_programs(0) - 1)
    def _():
        dwi_ref[...] = dwi[...].astype(BF16)
        dwo_ref[...] = dwo[...].astype(BF16)


def experts_pass(tokens, grads, weights, inner, outer):
    rows, width = tokens.shape
    block = 256
    row_spec = pl.BlockSpec((block, width), lambda i: (i, 0))
    count = inner.shape[0]
    gate_spec = pl.BlockSpec((block, count), lambda i: (i, 0))
    once = pl.Buffered(1)
    inner_spec = pl.BlockSpec(inner.shape, lambda i: (0, 0, 0), pipeline_mode=once)
    outer_spec = pl.BlockSpec(outer.shape, lambda i: (0, 0, 0), pipeline_mode=once)
    return pl.pallas_call(
        expert_kernel,
        grid=(rows // block,),
        in_specs=[row_spec, row_spec, gate_spec, inner_spec, outer_spec],
        out_specs=[row_spec, row_spec, gate_spec, inner_spec, outer_spec],
        out_shape=[
            jax.ShapeDtypeStruct((rows, width), BF16),
            jax.ShapeDtypeStruct((rows, width), BF16),
            jax.ShapeDtypeStruct((rows, count), F32),
            jax.ShapeDtypeStruct(inner.shape, BF16),
            jax.ShapeDtypeStruct(outer.shape, BF16),
        ],
        scratch_shapes=[
            pltpu.VMEM(inner.shape, F32),
            pltpu.VMEM(outer.shape, F32),
            pltpu.VMEM((block, count * EXPERT_H), BF16),
            pltpu.VMEM((block, 2 * count * EXPERT_H), BF16),
        ],
        compiler_params=pltpu.CompilerParams(vmem_limit_bytes=60 << 20),
        cost_estimate=pl.CostEstimate(
            flops=18 * count * rows * width * EXPERT_H,
            bytes_accessed=48 << 20,
            transcendentals=rows * count * EXPERT_H,
        ),
        name="experts",
    )(tokens, grads, weights, inner, outer)


MESH = pl.DeviceIdType.MESH
SLOW = 4
CHUNKS = 2


def ring_position(index, size):
    fast = size // SLOW
    row, column = lax.div(index, fast), lax.rem(index, fast)
    back = SLOW - 1 - row
    odd = lax.rem(back, 2)
    along = (column - 1) * (1 - odd) + (fast - 1 - column) * odd
    away = lax.div(column + fast - 2, fast - 1)
    return (1 - away) * row + away * (SLOW + back * (fast - 1) + along)


def ring_index(position, size):
    fast = size // SLOW
    away = lax.div(lax.div(position, SLOW) + fast - 2, fast - 1)
    rest = away * (position - SLOW)
    back, step = lax.div(rest, fast - 1), lax.rem(rest, fast - 1)
    odd = lax.rem(back, 2)
    column = (1 + step) * (1 - odd) + (fast - 1 - step) * odd
    return (1 - away) * position * fast + away * ((SLOW - 1 - back) * fast + column)


class Ring:
    def __init__(self, size):
        self.size, self.steps = size, size // 2
        self.me = lax.axis_index("ctx")
        self.place = ring_position(self.me, size)

    def at(self, shift):
        return ring_index(lax.rem(self.place + shift + self.size, self.size), self.size)

    def toward(self, direction, distance):
        return self.at(distance if direction == 0 else -distance)

    def device(self, direction):
        return (self.toward(direction, 1), lax.axis_index("wsh"))

    def meet(self):
        barrier = pltpu.get_barrier_semaphore()
        for direction in range(2):
            pl.semaphore_signal(
                barrier, inc=1, device_id=self.device(direction), device_id_type=MESH
            )
        pl.semaphore_wait(barrier, 2)

    def chunks(self, direction, last):
        if not last:
            return range(CHUNKS)
        half = CHUNKS // 2
        return range(half) if direction == 0 else range(half, CHUNKS)


def rows_at(block, rows, chunk):
    part = rows // CHUNKS
    return pl.ds(pl.multiple_of(block * rows + chunk * part, part), part)


def ring_gather_kernel(size, count, *refs):
    locals_, outs = refs[:count], refs[count : 2 * count]
    send, recv, own = refs[2 * count :]
    ring = Ring(size)
    ring.meet()

    def copy(k, direction, step, chunk, block):
        rows = locals_[k].shape[0]
        source = (
            locals_[k].at[rows_at(0, rows, chunk)]
            if step == 0
            else outs[k].at[rows_at(block, rows, chunk)]
        )
        return pltpu.make_async_remote_copy(
            src_ref=source,
            dst_ref=outs[k].at[rows_at(block, rows, chunk)],
            send_sem=send.at[k, direction, step, chunk],
            recv_sem=recv.at[k, direction, step, chunk],
            device_id=ring.device(direction),
            device_id_type=MESH,
        )

    started = []
    kept = []
    for step in range(ring.steps):
        for chunk in range(CHUNKS):
            for direction in range(2):
                if step > 0:
                    for k in range(count):
                        block = ring.toward(1 - direction, step)
                        copy(k, direction, step - 1, chunk, block).wait_recv()
                if chunk in ring.chunks(direction, step == ring.steps - 1):
                    for k in range(count):
                        moved = copy(k, direction, step, chunk, ring.toward(1 - direction, step))
                        moved.start()
                        started.append(moved)
        if step == 0:
            for k in range(count):
                rows = locals_[k].shape[0]
                place = pl.ds(pl.multiple_of(ring.me * rows, rows), rows)
                kept.append(pltpu.make_async_copy(locals_[k], outs[k].at[place], own.at[k]))
                kept[-1].start()
    last = ring.steps - 1
    for direction in range(2):
        for chunk in ring.chunks(direction, True):
            for k in range(count):
                copy(k, direction, last, chunk, ring.toward(1 - direction, last + 1)).wait_recv()
    for moved in started:
        moved.wait_send()
    for moved in kept:
        moved.wait()


def ring_gather(arrays, size, identity, name):
    count = len(arrays)
    sems = pltpu.SemaphoreType.DMA((count, 2, size // 2, CHUNKS))
    return pl.pallas_call(
        functools.partial(ring_gather_kernel, size, count),
        in_specs=[pl.BlockSpec(memory_space=pltpu.VMEM)] * count,
        out_specs=[pl.BlockSpec(memory_space=pl.ANY)] * count,
        out_shape=[
            jax.ShapeDtypeStruct((size * a.shape[0],) + a.shape[1:], a.dtype) for a in arrays
        ],
        scratch_shapes=[sems, sems, pltpu.SemaphoreType.DMA((count,))],
        compiler_params=pltpu.CompilerParams(collective_id=identity, has_side_effects=True),
        cost_estimate=pl.CostEstimate(flops=0, bytes_accessed=100 << 20, transcendentals=0),
        name=name,
    )(*arrays)


def ring_scatter_kernel(size, count, *refs):
    parts, outs = refs[:count], refs[count : 2 * count]
    stages, lands = refs[2 * count : 3 * count], refs[3 * count : 4 * count]
    send, recv = refs[4 * count :]
    ring = Ring(size)
    ring.meet()

    def copy(k, direction, step, chunk):
        rows = outs[k].shape[0]
        if step == 0:
            source = parts[k].at[rows_at(ring.toward(direction, ring.steps), rows, chunk)]
        else:
            source = stages[k].at[direction, step - 1, rows_at(0, rows, chunk)]
        return pltpu.make_async_remote_copy(
            src_ref=source,
            dst_ref=lands[k].at[direction, step, rows_at(0, rows, chunk)],
            send_sem=send.at[k, direction, step, chunk],
            recv_sem=recv.at[k, direction, step, chunk],
            device_id=ring.device(direction),
            device_id_type=MESH,
        )

    started = []
    for step in range(ring.steps):
        for chunk in range(CHUNKS):
            for direction in range(2):
                for k in range(count):
                    rows = outs[k].shape[0]
                    if step == 0:
                        if chunk not in ring.chunks(direction, True):
                            continue
                    else:
                        here = rows_at(0, rows, chunk)
                        dest = ring.toward(direction, ring.steps - step)
                        total = parts[k][rows_at(dest, rows, chunk)]
                        if step > 1 or chunk in ring.chunks(direction, True):
                            copy(k, direction, step - 1, chunk).wait_recv()
                            landed = lands[k][direction, step - 1, here]
                            total = (total.astype(F32) + landed.astype(F32)).astype(total.dtype)
                        stages[k][direction, step - 1, here] = total
                    moved = copy(k, direction, step, chunk)
                    moved.start()
                    started.append(moved)
    last = ring.steps - 1
    for chunk in range(CHUNKS):
        for k in range(count):
            rows = outs[k].shape[0]
            here = rows_at(0, rows, chunk)
            total = parts[k][rows_at(ring.me, rows, chunk)].astype(F32)
            for direction in range(2):
                copy(k, direction, last, chunk).wait_recv()
                total += lands[k][direction, last, here].astype(F32)
            outs[k][here] = total
    for moved in started:
        moved.wait_send()


def ring_scatter(arrays, size, identity, name):
    count, steps = len(arrays), size // 2
    sems = pltpu.SemaphoreType.DMA((count, 2, steps, CHUNKS))
    blocks = [(a.shape[0] // size,) + a.shape[1:] for a in arrays]
    vmem = pl.BlockSpec(memory_space=pltpu.VMEM)
    return pl.pallas_call(
        functools.partial(ring_scatter_kernel, size, count),
        in_specs=[vmem] * count,
        out_specs=[vmem] * count,
        out_shape=[jax.ShapeDtypeStruct(b, F32) for b in blocks],
        scratch_shapes=[
            pltpu.VMEM((2, steps - 1) + b, a.dtype) for a, b in zip(arrays, blocks)
        ]
        + [pltpu.VMEM((2, steps) + b, a.dtype) for a, b in zip(arrays, blocks)]
        + [sems, sems],
        compiler_params=pltpu.CompilerParams(
            collective_id=identity, has_side_effects=True, vmem_limit_bytes=48 << 20
        ),
        cost_estimate=pl.CostEstimate(flops=0, bytes_accessed=100 << 20, transcendentals=0),
        name=name,
    )(*arrays)


FUSED_BYTES = 52 << 20


def fused_kernel(
    size, x_in, gate_in, g_hbm, wi_hbm, wo_hbm, back_out, gate_out, mix_hbm, dwi_hbm, dwo_hbm,
    x, gates, g, wi, wo, rows, mid, part, gate_part, land, gate_land,
    out_send, out_recv, sum_send, sum_recv, local,
):
    ring = Ring(size)
    steps, me = ring.steps, ring.me
    block, width = x_in.shape
    count = wi.shape[0]
    experts = gate_in.shape[0]
    tile = 256
    loads = [
        pltpu.make_async_copy(a, b, local.at[i])
        for i, (a, b) in enumerate(((wi_hbm, wi), (g_hbm, g), (wo_hbm, wo)))
    ]
    for load in loads:
        load.start()
    ring.meet()
    whole_arrays, own_arrays = (x, gates), (x_in, gate_in)

    def remote(source, target, send, recv, direction):
        return pltpu.make_async_remote_copy(
            src_ref=source,
            dst_ref=target,
            send_sem=send,
            recv_sem=recv,
            device_id=ring.device(direction),
            device_id_type=MESH,
        )

    def spread(k, direction, step, chunk, origin, first=False):
        height = own_arrays[k].shape[0]
        at = rows_at(origin, height, chunk)
        source = own_arrays[k].at[rows_at(0, height, chunk)] if first else whole_arrays[k].at[at]
        return remote(
            source,
            whole_arrays[k].at[at],
            out_send.at[k, direction, step, chunk],
            out_recv.at[k, direction, step, chunk],
            direction,
        )

    for chunk in range(CHUNKS):
        for direction in range(2):
            for k in range(2):
                spread(k, direction, 0, chunk, me, True).start()
    x[pl.ds(pl.multiple_of(me * block, block), block), :] = x_in[...]
    gates[pl.ds(pl.multiple_of(me * experts, experts), experts), :] = gate_in[...]
    for load in loads:
        load.wait()

    lanes = lax.broadcasted_iota(jnp.int32, (block, experts), 1)

    def backward_rows(origin):
        at = pl.ds(pl.multiple_of(origin * block, block), block)
        gate_at = pl.ds(pl.multiple_of(origin * experts, experts), experts)
        turned = gates[gate_at, :].T
        picked = jnp.zeros((block, experts), F32)
        grad = g[at, :]
        for e in range(count):
            mine = lanes == me * count + e
            weight = jnp.sum(jnp.where(mine, turned, 0.0), axis=1, keepdims=True)
            gate_sum = jnp.zeros((block, 1), F32)
            for low in range(0, EXPERT_H, tile):
                gate = dot(x[at, :], wi[e, :, low : low + tile])
                up = dot(x[at, :], wi[e, :, EXPERT_H + low : EXPERT_H + low + tile])
                inward = dot_nt(grad, wo[e, low : low + tile, :])
                sigmoid = 1.0 / (1.0 + jnp.exp(-gate))
                silu = gate * sigmoid
                hidden = (silu * up).astype(BF16).astype(F32)
                gate_sum += jnp.sum(hidden * inward, axis=1, keepdims=True)
                hidden_grad = weight * inward
                to = e * EXPERT_H + low
                mid[at, to : to + tile] = (weight * hidden).astype(BF16)
                to = 2 * e * EXPERT_H + low
                rows[at, to : to + tile] = (
                    hidden_grad * up * sigmoid * (1.0 + gate * (1.0 - sigmoid))
                ).astype(BF16)
                to += EXPERT_H
                rows[at, to : to + tile] = (hidden_grad * silu).astype(BF16)
            picked = jnp.where(mine, gate_sum, picked)
        gate_part[gate_at, :] = picked.T

        @pl.loop(0, width // tile)
        def _(t):
            to = pl.ds(pl.multiple_of(t * tile, tile), tile)
            back = 0.0
            for e in range(count):
                inner = rows[at, 2 * e * EXPERT_H : 2 * (e + 1) * EXPERT_H]
                back += dot_nt(inner, wi[e, to, :])
            part[at, to] = back.astype(BF16)

    def visit(j, carry):
        step = lax.div(j + 1, 2)
        odd = lax.rem(j, 2)

        @pl.when((odd == 1) & (j < size - 1))
        def _():
            for chunk in range(CHUNKS):
                for direction in range(2):
                    origin = ring.toward(1 - direction, step)
                    for k in range(2):
                        spread(k, direction, step - 1, chunk, origin).wait_recv()

                    def forward():
                        for k in range(2):
                            spread(k, direction, step, chunk, origin).start()

                    if chunk in ring.chunks(direction, True):
                        forward()
                    else:
                        pl.when(step < steps - 1)(forward)

        @pl.when(j == size - 1)
        def _():
            for direction in range(2):
                for chunk in ring.chunks(direction, True):
                    for k in range(2):
                        origin = ring.toward(1 - direction, steps)
                        spread(k, direction, steps - 1, chunk, origin).wait_recv()

        backward_rows(ring.at(step * (1 - 2 * odd)))
        return carry

    lax.fori_loop(0, size, visit, 0)

    parts, lands, outs = (part, gate_part), (land, gate_land), (back_out, gate_out)

    def inward_copy(k, direction, step, chunk):
        height = own_arrays[k].shape[0]
        dest = ring.toward(direction, steps - step)
        return remote(
            parts[k].at[rows_at(dest, height, chunk)],
            lands[k].at[direction, step, rows_at(0, height, chunk)],
            sum_send.at[k, direction, step, chunk],
            sum_recv.at[k, direction, step, chunk],
            direction,
        )

    def inward_step(step):
        for chunk in range(CHUNKS):
            for direction in range(2):
                near = chunk in ring.chunks(direction, True)
                if step == 0 and not near:
                    continue
                for k in range(2):
                    height = own_arrays[k].shape[0]
                    if step > 1 or (step == 1 and near):
                        inward_copy(k, direction, step - 1, chunk).wait_recv()
                        at = rows_at(ring.toward(direction, steps - step), height, chunk)
                        landed = lands[k][direction, step - 1, rows_at(0, height, chunk)]
                        both = parts[k][at, :].astype(F32) + landed.astype(F32)
                        parts[k][at, :] = both.astype(parts[k].dtype)
                    inward_copy(k, direction, step, chunk).start()

    def inner_gradient(t):
        to = pl.ds(pl.multiple_of(t * tile, tile), tile)
        for e in range(count):
            inner = rows[:, 2 * e * EXPERT_H : 2 * (e + 1) * EXPERT_H]
            wi[e, to, :] = dot_tn(x[:, to], inner).astype(BF16)

    def outer_gradient(t):
        e = lax.div(t, EXPERT_H // tile)
        low = lax.rem(t, EXPERT_H // tile)
        from_ = pl.ds(pl.multiple_of(t * tile, tile), tile)
        to = pl.ds(pl.multiple_of(low * tile, tile), tile)
        wo[e, to, :] = dot_tn(mid[:, from_], g[...]).astype(BF16)

    def mixture(origin):
        at = pl.ds(pl.multiple_of(origin * block, block), block)
        mixed = 0.0
        for e in range(count):
            mixed += dot(mid[at, e * EXPERT_H : (e + 1) * EXPERT_H], wo[e])
        x[at, :] = mixed.astype(BF16)

    tiles = width // tile
    cuts = [round(tiles * i / (steps - 1)) for i in range(steps)]
    stores = [
        pltpu.make_async_copy(a, b, local.at[i])
        for i, (a, b) in enumerate(((wi, dwi_hbm), (x, mix_hbm), (wo, dwo_hbm)))
    ]
    for step in range(steps):
        inward_step(step)
        if step < steps - 1:
            pl.loop(cuts[step], cuts[step + 1])(inner_gradient)
        else:
            stores[0].start()
            for k in range(2):
                for direction in range(2):
                    for hop in range(steps):
                        for chunk in ring.chunks(direction, hop == steps - 1):
                            spread(k, direction, hop, chunk, me, hop == 0).wait_send()
            pl.loop(0, size)(mixture)
            stores[1].start()
            pl.loop(0, count * EXPERT_H // tile)(outer_gradient)
            stores[2].start()
    for chunk in range(CHUNKS):
        for k in range(2):
            height = own_arrays[k].shape[0]
            here = rows_at(0, height, chunk)
            total = parts[k][rows_at(me, height, chunk), :].astype(F32)
            for direction in range(2):
                inward_copy(k, direction, steps - 1, chunk).wait_recv()
                total += lands[k][direction, steps - 1, here].astype(F32)
            outs[k][here, :] = total
    for k in range(2):
        for direction in range(2):
            for step in range(steps):
                for chunk in ring.chunks(direction, step == 0):
                    inward_copy(k, direction, step, chunk).wait_send()
    for store in stores:
        store.wait()


def fused_scratch(tokens, gates, inner, outer, size):
    block, width = tokens.shape
    count, steps = inner.shape[0], size // 2
    rows, gate_rows = size * block, size * gates.shape[0]
    return [
        pltpu.VMEM((rows, width), BF16),
        pltpu.VMEM((gate_rows, block), F32),
        pltpu.VMEM((rows, width), BF16),
        pltpu.VMEM(inner.shape, BF16),
        pltpu.VMEM(outer.shape, BF16),
        pltpu.VMEM((rows, 2 * count * EXPERT_H), BF16),
        pltpu.VMEM((rows, count * EXPERT_H), BF16),
        pltpu.VMEM((rows, width), BF16),
        pltpu.VMEM((gate_rows, block), F32),
        pltpu.VMEM((2, steps, block, width), BF16),
        pltpu.VMEM((2, steps) + gates.shape, F32),
    ]


def fused_fits(*shapes):
    return sum(r.dtype.itemsize * functools.reduce(lambda a, b: a * b, r.shape) for r in fused_scratch(*shapes)) <= FUSED_BYTES


def fused_experts(tokens, gates, grads, inner, outer, size, identity):
    block, width = tokens.shape
    count, steps = inner.shape[0], size // 2
    rows = size * block
    vmem, hbm = pl.BlockSpec(memory_space=pltpu.VMEM), pl.BlockSpec(memory_space=pl.ANY)
    sems = pltpu.SemaphoreType.DMA((2, 2, steps, CHUNKS))
    return pl.pallas_call(
        functools.partial(fused_kernel, size),
        in_specs=[vmem, vmem, hbm, hbm, hbm],
        out_specs=[vmem, vmem, hbm, hbm, hbm],
        out_shape=[
            jax.ShapeDtypeStruct(tokens.shape, F32),
            jax.ShapeDtypeStruct(gates.shape, F32),
            jax.ShapeDtypeStruct((rows, width), BF16),
            jax.ShapeDtypeStruct(inner.shape, BF16),
            jax.ShapeDtypeStruct(outer.shape, BF16),
        ],
        scratch_shapes=fused_scratch(tokens, gates, inner, outer, size)
        + [sems] * 4
        + [pltpu.SemaphoreType.DMA((3,))],
        compiler_params=pltpu.CompilerParams(
            collective_id=identity, has_side_effects=True, vmem_limit_bytes=63 << 20
        ),
        cost_estimate=pl.CostEstimate(
            flops=18 * count * rows * width * EXPERT_H,
            bytes_accessed=300 << 20,
            transcendentals=rows * count * EXPERT_H,
        ),
        name="fused_experts",
    )(tokens, gates, grads, inner, outer)


EXTRA = 16


def reduce_kernel(
    size, shards, lhs, rhs, small, out, part, cores, lines, total, stage, land, held,
    core_send, core_recv, line_send, line_recv, ring_send, ring_recv, all_send, all_recv,
):
    ring = Ring(size)
    steps, height = ring.steps, shards // 2
    spot = lax.axis_index("wsh")
    core, row = lax.rem(spot, 2), lax.div(spot, 2)
    ctx = ring.me
    slot_rows, width = total.shape[1], total.shape[2]
    shard_rows = slot_rows - EXTRA
    split = width // CHUNKS
    mate = (ctx, row * 2 + 1 - core)
    above = (ctx, lax.rem(row + 1, height) * 2 + core)
    below = (ctx, lax.rem(row + height - 1, height) * 2 + core)

    barrier = pltpu.get_barrier_semaphore()
    for device in (mate, above, below, ring.device(0), ring.device(1)):
        pl.semaphore_signal(barrier, inc=1, device_id=device, device_id_type=MESH)
    pl.semaphore_wait(barrier, 5)

    order = [steps]
    for distance in range(steps - 1, 0, -1):
        order += [distance, -distance]
    order.append(0)
    slot_of = {shift: i for i, shift in enumerate(order)}
    slot_of[-steps] = 0
    blocks = [ring.at(shift) for shift in order]
    started = []

    def begin(copy):
        copy.start()
        started.append(copy)

    def remote(source, target, send, recv, device):
        return pltpu.make_async_remote_copy(
            src_ref=source,
            dst_ref=target,
            send_sem=send,
            recv_sem=recv,
            device_id=device,
            device_id_type=MESH,
        )

    def to_mate(i, y):
        return remote(
            part.at[i, y * 2 + 1 - core], cores.at[i, y], core_send.at[i, y], core_recv.at[i, y], mate
        )

    def to_line(i, t):
        shard = lax.rem(row + 2 * height - 1 - t, height) * 2 + core
        return remote(
            part.at[i, shard], lines.at[i, t], line_send.at[i, t], line_recv.at[i, t], above
        )

    def form(i):
        at = pl.multiple_of(blocks[i] * width, width)
        side = lax.div(blocks[i] * width, lhs.shape[1] + 2 * KEY_HEADS * HEAD_SIZE)

        @pl.loop(0, shards)
        def _(w):
            rows = pl.ds(pl.multiple_of(w * shard_rows, shard_rows), shard_rows)
            product = dot(lhs[side, rows, :], rhs[:, pl.ds(at, width)])
            part[i, w, :shard_rows, :] = product.astype(BF16)
            part[i, w, shard_rows:, :] = small[w, :, pl.ds(at, width)]

        for y in range(height):
            begin(to_mate(i, y))

    def add_cores(i):
        for y in range(height):
            to_mate(i, y).wait_recv()
            both = part[i, y * 2 + core].astype(F32) + cores[i, y].astype(F32)
            part[i, y * 2 + core] = both.astype(BF16)
        begin(to_line(i, 0))

    for i in range(size):
        form(i)
        if i > 0:
            add_cores(i - 1)
    add_cores(size - 1)
    for t in range(1, height - 1):
        for i in range(size):
            to_line(i, t - 1).wait_recv()
            shard = lax.rem(row + 2 * height - 1 - t, height) * 2 + core
            both = part[i, shard].astype(F32) + lines[i, t - 1].astype(F32)
            part[i, shard] = both.astype(BF16)
            begin(to_line(i, t))

    def finish_line(i):
        to_line(i, height - 2).wait_recv()
        total[i] = part[i, spot].astype(F32) + lines[i, height - 2].astype(F32)

    def columns(chunk):
        return pl.ds(chunk * split, split)

    def around(direction, step, chunk):
        return remote(
            stage.at[direction, step, :, columns(chunk)],
            land.at[direction, step, :, columns(chunk)],
            ring_send.at[direction, step, chunk],
            ring_recv.at[direction, step, chunk],
            ring.device(direction),
        )

    for step in range(steps):
        reach = steps - step
        for i in sorted({slot_of[reach], slot_of[-reach]}):
            finish_line(i)
        for chunk in range(CHUNKS):
            for direction in range(2):
                if step == 0 and chunk not in ring.chunks(direction, True):
                    continue
                at = columns(chunk)
                value = total[slot_of[reach if direction == 0 else -reach], :, at]
                if step > 1 or (step == 1 and chunk in ring.chunks(direction, True)):
                    around(direction, step - 1, chunk).wait_recv()
                    value += land[direction, step - 1, :, at].astype(F32)
                stage[direction, step, :, at] = value.astype(BF16)
                begin(around(direction, step, chunk))

    def onward(direction, step, chunk, block):
        return remote(
            held.at[block, :, columns(chunk)],
            held.at[block, :, columns(chunk)],
            all_send.at[direction, step, chunk],
            all_recv.at[direction, step, chunk],
            ring.device(direction),
        )

    def put(block, chunk):
        at = pl.ds(pl.multiple_of(block * width + chunk * split, split), split)
        out[:, at] = held[block, :, columns(chunk)].astype(F32)

    own = slot_of[0]
    finish_line(own)
    for chunk in range(CHUNKS):
        at = columns(chunk)
        value = total[own, :, at]
        for direction in range(2):
            around(direction, steps - 1, chunk).wait_recv()
            value += land[direction, steps - 1, :, at].astype(F32)
        held[ctx, :, at] = value.astype(BF16)
        for direction in range(2):
            begin(onward(direction, 0, chunk, ctx))
    for chunk in range(CHUNKS):
        put(ctx, chunk)
    for step in range(1, steps + 1):
        for chunk in range(CHUNKS):
            for direction in range(2):
                if step == steps and chunk not in ring.chunks(direction, True):
                    continue
                block = ring.toward(1 - direction, step)
                onward(direction, step - 1, chunk, block).wait_recv()
                if step < steps and chunk in ring.chunks(direction, step == steps - 1):
                    begin(onward(direction, step, chunk, block))
                put(block, chunk)
    for copy in started:
        copy.wait_send()


def reduce_grads(lhs, rhs, small, size, shards, identity):
    steps, height = size // 2, shards // 2
    columns = rhs.shape[1]
    width, rows = columns // size, lhs.shape[1] // shards + EXTRA
    vmem = pl.BlockSpec(memory_space=pltpu.VMEM)
    dma = pltpu.SemaphoreType.DMA
    return pl.pallas_call(
        functools.partial(reduce_kernel, size, shards),
        in_specs=[vmem] * 3,
        out_specs=vmem,
        out_shape=jax.ShapeDtypeStruct((rows, columns), F32),
        scratch_shapes=[
            pltpu.VMEM((size, shards, rows, width), BF16),
            pltpu.VMEM((size, height, rows, width), BF16),
            pltpu.VMEM((size, height - 1, rows, width), BF16),
            pltpu.VMEM((size, rows, width), F32),
            pltpu.VMEM((2, steps, rows, width), BF16),
            pltpu.VMEM((2, steps, rows, width), BF16),
            pltpu.VMEM((size, rows, width), BF16),
            dma((size, height)),
            dma((size, height)),
            dma((size, height - 1)),
            dma((size, height - 1)),
        ]
        + [dma((2, steps, CHUNKS))] * 4,
        compiler_params=pltpu.CompilerParams(
            collective_id=identity, has_side_effects=True, vmem_limit_bytes=62 << 20
        ),
        cost_estimate=pl.CostEstimate(
            flops=2 * lhs.shape[1] * lhs.shape[2] * columns,
            bytes_accessed=300 << 20,
            transcendentals=0,
        ),
        name="reduce_grads",
    )(lhs, rhs, small)


def on_device(
    layer_input,
    attention_gain,
    query_weight,
    key_matrix,
    value_matrix,
    output_weight,
    expert_gain,
    router_weight,
    expert_inner,
    expert_outer,
    document_lengths,
    token_places,
    expert_routes,
    cotangent,
):
    group_devices = lax.axis_size("ctx")
    ctx_index = lax.axis_index("ctx")
    token_rows = layer_input.shape[1]
    experts = router_weight.shape[1]
    own_experts = expert_inner.shape[0]
    key_value_width = KEY_HEADS * HEAD_SIZE

    def gather(shard, axis=0):
        return lax.all_gather(shard, "wsh", axis=axis, tiled=True)

    projected = 2 * key_value_width + query_weight.shape[1]
    small = jnp.concatenate([attention_gain[:, None], expert_gain[:, None], router_weight], axis=1)
    small = jnp.pad(small, ((0, 0), (0, -small.shape[1] % 128)))
    first_weights = gather(
        jnp.concatenate([query_weight, key_matrix, value_matrix, small], axis=1)
    )
    whole_qkv = first_weights[:, :projected]
    gain_one = first_weights[:, projected].astype(F32)
    gain_two = first_weights[:, projected + 1].astype(F32)
    whole_router = first_weights[:, projected + 2 : projected + 2 + experts]
    whole_output = gather(output_weight)
    whole_inner = gather(expert_inner, 1)
    whole_outer = gather(expert_outer, 1)
    (all_grads,) = ring_gather([cotangent[0]], group_devices, 6, "gather_grads")

    places_all = token_places[0]
    key_documents, key_offsets = locate(document_lengths[0], places_all)
    first_row = ctx_index * token_rows
    query_places = lax.dynamic_slice_in_dim(places_all, first_row, token_rows)
    query_documents = lax.dynamic_slice_in_dim(key_documents, first_row, token_rows)
    query_offsets = lax.dynamic_slice_in_dim(key_offsets, first_row, token_rows)
    marks = (
        key_documents[:, None],
        places_all[:, None],
        query_documents[None, :],
        query_places[None, :],
    )
    cosine_rows, sine_table = angles_for(query_offsets)

    own_input, all_grads = lax.optimization_barrier((layer_input[0], all_grads))
    inputs_f = own_input.astype(F32)
    inverse_one = rms_inverse(inputs_f)
    normed_one = (inputs_f * inverse_one * gain_one).astype(BF16)
    pre = dot(normed_one, whole_qkv)
    query_pre = pre[:, : -2 * key_value_width]
    key_pre = pre[:, -2 * key_value_width : -key_value_width]
    keys = (
        apply_rotation(key_pre.reshape(token_rows, KEY_HEADS, HEAD_SIZE), cosine_rows, sine_table)
        .astype(BF16)
        .reshape(token_rows, key_value_width)
    )
    values = pre[:, -key_value_width:].astype(BF16)
    all_keys, all_values = ring_gather([keys, values], group_devices, 1, "gather_keys")
    queries = (
        apply_rotation(
            query_pre.reshape(token_rows, QUERY_HEADS, HEAD_SIZE), cosine_rows, sine_table
        ).astype(BF16)
        * SCALE
    ).reshape(token_rows, QUERY_HEADS * HEAD_SIZE)
    spread_queries = spread_heads(queries)
    spread_attended, lse = attend(spread_queries, all_keys, all_values, marks)
    attended_f = gather_heads(spread_attended)
    attended = attended_f.astype(BF16)
    residual = inputs_f + dot(attended, whole_output)
    inverse_two = rms_inverse(residual)
    normed_two = (residual * inverse_two * gain_two).astype(BF16)
    logits = dot(normed_two, whole_router)
    expert_ids = jnp.arange(experts, dtype=jnp.int32)
    routed = jnp.any(expert_routes[0][:, :, None] == expert_ids[None, None, :], axis=1)
    gates = jax.nn.softmax(jnp.where(routed, logits, -jnp.inf), axis=-1)

    turned_gates = gates.T
    if fused_fits(normed_two, turned_gates, whole_inner, whole_outer, group_devices):
        back_sum, gate_grad, mixed, inner_grad, outer_grad = fused_experts(
            normed_two, turned_gates, all_grads, whole_inner, whole_outer, group_devices, 7
        )
    else:
        all_tokens, all_gates = ring_gather([normed_two, turned_gates], group_devices, 2, "gather_tokens")
        own_gates = (
            lax.dynamic_slice_in_dim(
                all_gates.reshape(group_devices, experts, token_rows),
                ctx_index * own_experts,
                own_experts,
                axis=1,
            )
            .transpose(0, 2, 1)
            .reshape(group_devices * token_rows, own_experts)
        )
        mixed, back_rows, own_gate_grad, inner_grad, outer_grad = experts_pass(
            all_tokens, all_grads, own_gates, whole_inner, whole_outer
        )
        placed = lax.dynamic_update_slice_in_dim(
            jnp.zeros((group_devices, experts, token_rows), F32),
            own_gate_grad.reshape(group_devices, token_rows, own_experts).transpose(0, 2, 1),
            ctx_index * own_experts,
            axis=1,
        ).reshape(group_devices * experts, token_rows)
        back_sum, gate_grad = ring_scatter([back_rows, placed], group_devices, 3, "scatter_rows")
    gate_grad = gate_grad.T
    out_grad = cotangent[0].astype(F32)
    logit_grad = (
        gates * (gate_grad - jnp.sum(gates * gate_grad, axis=-1, keepdims=True))
    ).astype(BF16)
    router_grad = dot_tn(normed_two, logit_grad)
    normed_two_grad = dot_nt(logit_grad, whole_router) + back_sum
    gain_two_grad, residual_back = norm_backward(residual, inverse_two, gain_two, normed_two_grad)
    residual_grad = out_grad + residual_back
    branch_grad = residual_grad.astype(BF16)
    attended_grad = dot_nt(branch_grad, whole_output).astype(BF16)
    delta = jnp.sum(
        (attended_grad.astype(F32) * attended_f).reshape(token_rows, QUERY_HEADS, HEAD_SIZE), axis=-1
    ).T.reshape(PAIRS, PAIR_HEADS, 1, token_rows)
    spread_grads = spread_heads(attended_grad)
    spread_query_grad, key_part, value_part = attend_back(
        spread_queries,
        spread_queries.transpose(0, 1, 3, 2),
        spread_grads,
        spread_grads.transpose(0, 1, 3, 2),
        all_keys,
        all_values,
        lse,
        delta,
        marks,
    )
    key_grad, value_grad = ring_scatter([key_part, value_part], group_devices, 4, "scatter_keys")
    def scatter(grad, dim=0):
        return lax.psum_scatter(grad.astype(BF16), "wsh", scatter_dimension=dim, tiled=True)

    inner_out = scatter(inner_grad, 1)
    outer_out = scatter(outer_grad, 1)
    mixed, inner_out, outer_out, key_grad, value_grad = lax.optimization_barrier(
        (mixed, inner_out, outer_out, key_grad, value_grad)
    )
    mixture = lax.psum_scatter(mixed, "ctx", scatter_dimension=0, tiled=True)
    value_grad = value_grad.astype(BF16)
    query_pre_grad = (
        reverse_rotation(
            (gather_heads(spread_query_grad) * SCALE).reshape(token_rows, QUERY_HEADS, HEAD_SIZE),
            cosine_rows,
            sine_table,
        )
        .reshape(token_rows, QUERY_HEADS * HEAD_SIZE)
        .astype(BF16)
    )
    key_pre_grad = (
        reverse_rotation(
            key_grad.reshape(token_rows, KEY_HEADS, HEAD_SIZE), cosine_rows, sine_table
        )
        .reshape(token_rows, key_value_width)
        .astype(BF16)
    )
    pre_grad = jnp.concatenate([query_pre_grad, key_pre_grad, value_grad], axis=1)
    normed_one_grad = dot_nt(pre_grad, whole_qkv)
    gain_one_grad, input_back = norm_backward(inputs_f, inverse_one, gain_one, normed_one_grad)
    input_grad = residual_grad + input_back

    shards = lax.axis_size("wsh")
    shard_rows = query_weight.shape[0]
    columns = 2 * query_weight.shape[1] + 2 * key_value_width
    marks_small = jnp.concatenate(
        [gain_one_grad[None], gain_two_grad[None], router_grad.T], axis=0
    ).astype(BF16)
    small_count = marks_small.shape[0]
    small_rows = marks_small.reshape(small_count, shards, shard_rows).transpose(1, 0, 2)
    small_rows = small_rows.reshape(shards, small_count * shard_rows)
    across = -(-small_count * shard_rows // EXTRA // 128) * 128
    small_rows = jnp.pad(small_rows, ((0, 0), (0, EXTRA * across - small_rows.shape[1])))
    small_rows = jnp.pad(
        small_rows.reshape(shards, EXTRA, across), ((0, 0), (0, 0), (0, columns - across))
    )
    summed = reduce_grads(
        jnp.stack([normed_one.T, attended.T]),
        jnp.concatenate([pre_grad, branch_grad], axis=1),
        small_rows,
        group_devices,
        shards,
        5,
    )
    mixture, summed = lax.optimization_barrier((mixture, summed))
    layer_output = (residual + mixture.astype(F32)).astype(BF16)
    small_out = summed[shard_rows:, :across].reshape(-1)[: small_count * shard_rows]
    small_out = small_out.reshape(small_count, shard_rows)
    ends = [0]
    for shard in (query_weight, key_matrix, value_matrix, output_weight):
        ends.append(ends[-1] + shard.shape[1])
    query_out, key_out, value_out, output_out = (
        summed[:shard_rows, start:end] for start, end in zip(ends, ends[1:])
    )
    return (
        layer_output[None],
        input_grad[None],
        small_out[0],
        query_out,
        key_out,
        value_out,
        output_out,
        small_out[1],
        small_out[2:].T,
        inner_out.astype(F32),
        outer_out.astype(F32),
    )


def solution(mesh):
    tokens = P("wsh", "ctx", None)
    shard, expert = P("wsh", None), P("ctx", "wsh", None)
    return jax.shard_map(
        on_device,
        mesh=mesh,
        in_specs=(
            tokens,
            P("wsh"),
            shard,
            shard,
            shard,
            shard,
            P("wsh"),
            shard,
            expert,
            expert,
            shard,
            shard,
            tokens,
            tokens,
        ),
        out_specs=(
            tokens,
            tokens,
            P("wsh"),
            shard,
            shard,
            shard,
            shard,
            P("wsh"),
            shard,
            expert,
            expert,
        ),
        check_vma=False,
    )
```
